32 devices in a mesh: blk: 8 (over y, x, core), table: 4 (over z).
Axes of the slice: x: 2, y: 2, z: 4, core: 2. Of those that a mesh axis runs over, the one named last changes fastest.
Arguments:
- queries: bfloat16 [16384, 256], P(('blk', 'table')), may hold values from -20 to 20
- items: bfloat16 [16384, 256], P(('blk', 'table')), may hold values from -4.8 to 4.8
- positives: int32 [16384], P(('blk', 'table')), may hold values from 0 to 511
- item_owner: int32 [16384, 1], P(('blk', 'table')), may hold values from 0 to 31; in each aligned block of 512 rows (0 to 511, 512 to 1023, ...) at most 48 rows name the same one
- item_row: int32 [16384], P(('blk', 'table')), may hold values from 0 to 16383
Outputs:
- query_grad: bfloat16 [16384, 256], P(('blk', 'table'))
- item_grad: bfloat16 [16384, 256], P(('blk', 'table'))
- table_grad: bfloat16 [524288, 256], P(('blk', 'table'))
The draws below stay inside these ranges and needn't reach their ends.
Inputs may be any that keep to these rules, and one draw needn't show every extreme that they name: `item_owner`: among the rows of one device, no owner is named more than 48 times, a bound that some block reaches.
All inputs are finite; a program needn't handle non-finite values.
Results may differ from the reference program's by a relative error of at most 0.0034.
Values may be sent and summed in bfloat16 or wider, within the bound.
No kernel may reach another device: no remote copies, remote signals or barrier semaphores. Data moves between devices by JAX's collectives and lax.ppermute only.
A program may use at most 64 MiB of HBM per device.

```python
import math
import jax
import jax.numpy as jnp
import numpy as np
from jax import lax

D = 256
ROWS_DEV = 16384
ITEMS_DEV = 512
WINDOW = 4
CAP = 48
BATCH = 16384
ROWS = 524288
N_BLK = 8
N_TABLE = 4
DEVICES = 32


def pair_draw(key):
    query_key = jax.random.fold_in(key, 101)
    item_key = jax.random.fold_in(key, 102)
    items_base = jnp.clip(jax.random.normal(item_key, (BATCH, D), jnp.float32), -4.0, 4.0)
    query_base = jnp.clip(jax.random.normal(query_key, (BATCH, D), jnp.float32), -4.0, 4.0)
    return (query_base, items_base)


def draw_queries(key, part):
    return pair_draw(key)[0].astype(jnp.bfloat16)


def draw_items(key, part):
    return pair_draw(key)[1].astype(jnp.bfloat16)


def plant(values, key, low, high):
    longest = values.shape.index(max(values.shape))
    spots = []
    for shift in (0, 1):
        where = [jax.random.randint(jax.random.fold_in(key, axis), (), 0, length) for axis, length in enumerate(values.shape)]
        where[longest] = (where[longest] + shift) % values.shape[longest]
        spots.append(tuple(where))
    return values.at[spots[0]].set(low).at[spots[1]].set(high)


def shared_out(own_key, own, number, rows, number_of, top, limit, slope):
    sequence = jax.random.permutation(own_key, number_of)
    packed, ordinary = load_shares(number_of, rows * top, limit, slope, True), load_shares(number_of, rows * top, limit, slope, False)
    places = jnp.arange(number_of)

    def named(tallies, offset_by):
        used = int((tallies > 0).sum())
        fixed = max(1, used // 4)
        shifted = fixed + (places - fixed + offset_by * (used - fixed)) % max(1, number_of - fixed)
        return jnp.zeros((number_of,), jnp.int32).at[sequence[jnp.where(places < fixed, places, shifted)]].set(jnp.asarray(tallies, jnp.int32))

    tallies = jnp.where(number % 4 == 0, named(packed, number // 4), named(ordinary, number - number // 4 - 1))
    mixed = jax.random.permutation(jax.random.fold_in(own, 3), number_of)
    giver, taker = mixed[0:number_of // 2 * 2:2], mixed[1:number_of // 2 * 2:2]
    margin = jnp.minimum(tallies[giver] - 1, limit - tallies[taker]) // 2
    margin = jnp.where((giver == sequence[0]) | (taker == sequence[0]) | (tallies[taker] == 0), 0, jnp.maximum(margin, 0))
    shifted = jax.random.randint(jax.random.fold_in(own, 4), (number_of // 2,), 0, 1 << 20) % (margin + 1)
    tallies = tallies.at[giver].add(-shifted).at[taker].add(shifted)
    labels = jnp.searchsorted(jnp.cumsum(tallies), jnp.arange(rows * top), side="right").astype(jnp.int32)
    listing = labels.reshape(top, rows).T
    listing = listing[jax.random.permutation(jax.random.fold_in(own, 1), rows)]
    offset_by = jax.random.randint(jax.random.fold_in(own, 2), (rows, 1), 0, top)
    return jnp.take_along_axis(listing, (jnp.arange(top)[None, :] + offset_by) % top, axis=1)


def load_shares(amount, total, bound, skew, full):
    weights = [(1 << 20) // math.isqrt(grade ** skew) + 1 for grade in range(1, amount + 1)]
    largest = bound if full else min(bound, max(-(-total // amount), total * weights[0] // sum(weights)))
    least = 1 if total - largest >= amount - 1 else 0
    holding, spare = [largest] + [least] * (amount - 1), total - largest - least * (amount - 1)
    while spare > 0:
        candidates = [i for i in range(1, amount) if holding[i] < largest] or [i for i in range(1, amount) if holding[i] < bound]
        mass, budget = sum([weights[i] for i in candidates]), spare
        for i in candidates:
            more = min(bound - holding[i], max(1, budget * weights[i] // mass), spare)
            holding[i] = holding[i] + more
            spare = spare - more
    return np.array(holding)


def setup_inputs(seed: int = 0) -> dict:
    streams_of = jax.random.split(jax.random.key(seed), 6)
    queries = draw_queries(jax.random.fold_in(streams_of[5], 71), 0)
    items = draw_items(jax.random.fold_in(streams_of[5], 71), 0)
    positives = plant(jax.random.randint(streams_of[2], (BATCH,), 0, ITEMS_DEV), jax.random.fold_in(streams_of[2], 1), 0, ITEMS_DEV - 1).astype(jnp.int32)
    item_owner_keys = jax.random.split(jax.random.fold_in(streams_of[3], 1), BATCH // ITEMS_DEV)
    item_owner_turns = jax.random.permutation(jax.random.fold_in(streams_of[3], 3), BATCH // ITEMS_DEV)
    item_owner = jax.vmap(lambda own, number: shared_out(jax.random.fold_in(streams_of[3], 2), own, number, ITEMS_DEV, DEVICES, 1, CAP, 2))(item_owner_keys, item_owner_turns).reshape((BATCH, 1))
    item_row = plant(jax.random.randint(streams_of[4], (BATCH,), 0, ROWS_DEV), jax.random.fold_in(streams_of[4], 1), 0, ROWS_DEV - 1).astype(jnp.int32)
    return dict(queries=queries, items=items, positives=positives, item_owner=item_owner, item_row=item_row)


def reference(queries, items, positives, item_owner, item_row):
    feature_width = queries.shape[1]
    logit_scale = 3.0 / math.sqrt(feature_width)
    grid_shape = (N_BLK, N_TABLE, ITEMS_DEV, feature_width)
    query_all = queries.reshape(grid_shape)
    items_all = items.reshape(grid_shape)
    positive_all = positives.reshape(N_BLK, N_TABLE, ITEMS_DEV)
    places = jnp.arange(ITEMS_DEV, dtype=jnp.int32)
    block_ids = jnp.arange(N_BLK * N_TABLE, dtype=jnp.int32)

    def scores_of(query_block, item_block):
        return logit_scale * jnp.dot(query_block.astype(jnp.float32), item_block.astype(jnp.float32).T, precision=lax.Precision.HIGHEST)

    def fetch(grid, row_block, column):
        return lax.dynamic_index_in_dim(lax.dynamic_index_in_dim(grid, row_block, 0, keepdims=False), column, 0, keepdims=False)

    def totals_one(block_id):
        row_block = (block_id // N_TABLE).astype(jnp.int32)
        column = (block_id % N_TABLE).astype(jnp.int32)
        query_block = fetch(query_all, row_block, column)
        scores = scores_of(query_block, fetch(items_all, row_block, column))
        top_now = lax.optimization_barrier(jnp.max(scores, axis=1))
        total_now = lax.optimization_barrier(jnp.sum(jnp.exp(scores - top_now[:, None]), axis=1))
        for offset in range(1, WINDOW):
            source = ((row_block - offset) % N_BLK).astype(jnp.int32)
            scores = scores_of(query_block, fetch(items_all, source, column))
            top_new = jnp.maximum(top_now, lax.optimization_barrier(jnp.max(scores, axis=1)))
            total_now = total_now * jnp.exp(top_now - top_new) + lax.optimization_barrier(jnp.sum(jnp.exp(scores - top_new[:, None]), axis=1))
            top_now = top_new
        return top_now + jnp.log(total_now)
    log_total = lax.map(totals_one, block_ids).reshape(N_BLK, N_TABLE, ITEMS_DEV)

    def weights_of(query_block, item_block, totals, positive_rows, offset):
        weights = jnp.exp(scores_of(query_block, item_block) - totals[:, None])
        if offset == 0:
            weights = weights - (positive_rows[:, None] == places[None, :]).astype(weights.dtype)
        return lax.optimization_barrier(weights.astype(jnp.bfloat16)).astype(jnp.float32)

    def query_side(block_id):
        row_block = (block_id // N_TABLE).astype(jnp.int32)
        column = (block_id % N_TABLE).astype(jnp.int32)
        query_block = fetch(query_all, row_block, column)
        totals = fetch(log_total, row_block, column)
        positive_rows = fetch(positive_all, row_block, column)
        summed = jnp.zeros((ITEMS_DEV, feature_width), jnp.float32)
        for offset in range(WINDOW):
            source = ((row_block - offset) % N_BLK).astype(jnp.int32)
            item_block = fetch(items_all, source, column)
            weights = weights_of(query_block, item_block, totals, positive_rows, offset)
            summed = summed + jnp.dot(weights, item_block.astype(jnp.float32), precision=lax.Precision.HIGHEST)
        return (logit_scale * summed).astype(jnp.bfloat16)

    def item_side(block_id):
        row_block = (block_id // N_TABLE).astype(jnp.int32)
        column = (block_id % N_TABLE).astype(jnp.int32)
        item_block = fetch(items_all, row_block, column)
        summed = jnp.zeros((ITEMS_DEV, feature_width), jnp.float32)
        for offset in range(WINDOW):
            target = ((row_block + offset) % N_BLK).astype(jnp.int32)
            query_block = fetch(query_all, target, column)
            weights = weights_of(query_block, item_block, fetch(log_total, target, column), fetch(positive_all, target, column), offset)
            summed = summed + jnp.dot(weights.T, query_block.astype(jnp.float32), precision=lax.Precision.HIGHEST)
        return (logit_scale * summed).astype(jnp.bfloat16)
    query_grad = lax.map(query_side, block_ids).reshape(BATCH, feature_width)
    item_grad = lax.map(item_side, block_ids).reshape(BATCH, feature_width)
    grad_rows = item_grad.astype(jnp.float32)
    owners = item_owner[:, 0]

    def one_owner(owner):
        target = jnp.where(owners == owner, item_row, ROWS_DEV).astype(jnp.int32)
        summed = jnp.zeros((ROWS_DEV, feature_width), jnp.float32).at[target].add(grad_rows, mode='drop')
        return summed.astype(jnp.bfloat16)
    table_grad = lax.map(one_owner, jnp.arange(DEVICES, dtype=jnp.int32)).reshape(ROWS, feature_width)
    return (query_grad, item_grad, table_grad)
```

```python
import functools
import math

import jax
import jax.numpy as jnp
from jax import lax
from jax.experimental import pallas as pl
from jax.experimental.pallas import tpu as pltpu
from jax.sharding import PartitionSpec as P

ROWS_DEV = 16384
LANES = 128
SUB = 256
NT = (((1,), (1,)), ((), ()))
TN = (((0,), (0,)), ((), ()))


def moved(block, axis, target_of):
    count = lax.axis_size(axis)
    return lax.ppermute(block, axis, [(i, target_of(i) % count) for i in range(count)])


def vmem():
    return pl.BlockSpec(memory_space=pltpu.VMEM)


def call(body, out_shape, args, flops=0, trans=0):
    moved_bytes = sum(a.size * a.dtype.itemsize for a in args)
    outs = out_shape if isinstance(out_shape, (tuple, list)) else (out_shape,)
    moved_bytes += sum(math.prod(o.shape) * o.dtype.itemsize for o in outs)
    specs = [vmem() for _ in outs]
    return pl.pallas_call(
        body,
        out_shape=out_shape,
        in_specs=[vmem() for _ in args],
        out_specs=specs if isinstance(out_shape, (tuple, list)) else specs[0],
        cost_estimate=pl.CostEstimate(flops=flops, bytes_accessed=moved_bytes, transcendentals=trans),
    )(*args)


def iota(shape, dim, dtype=jnp.int32):
    value = lax.broadcasted_iota(jnp.int32, shape, dim)
    return value if dtype == jnp.int32 else value.astype(dtype)


def column(row):
    wide = jnp.broadcast_to(row, (LANES, LANES))
    return jnp.transpose(wide)


def route_kernel(devices, capacity, owner_ref, row_ref, pick_ref, ids_ref):
    size = owner_ref.shape[1]
    owner = owner_ref[...].astype(jnp.float32)
    rank = jnp.zeros((1, size), jnp.float32)
    for base in range(0, size, LANES):
        col = column(owner[:, base : base + LANES])
        col = jnp.concatenate([col] * (size // LANES), axis=1)
        here = iota((LANES, size), 0) + base
        hit = (col == owner) & (here < iota((LANES, size), 1))
        rank = rank + jnp.sum(jnp.where(hit, 1.0, 0.0), axis=0, keepdims=True)
    slot = owner * float(capacity) + rank
    slots = devices * capacity
    for base in range(0, slots, LANES):
        here = iota((LANES, size), 0, jnp.float32) + float(base)
        pick_ref[base : base + LANES, :] = jnp.where(here == slot, 1.0, 0.0).astype(jnp.bfloat16)
    row = row_ref[...]
    high = (lax.shift_right_logical(row, 7) + 1).astype(jnp.float32)
    low = (row & 127).astype(jnp.float32)
    mine = iota((devices, size), 0, jnp.float32) == owner
    place = jnp.where(iota((LANES, size), 0, jnp.float32) == rank, 1.0, 0.0).astype(jnp.bfloat16)
    high = jnp.where(mine, high, 0.0).astype(jnp.bfloat16)
    low = jnp.where(mine, low, 0.0).astype(jnp.bfloat16)
    high = lax.dot_general(high, place, NT, preferred_element_type=jnp.float32)
    low = lax.dot_general(low, place, NT, preferred_element_type=jnp.float32)
    value = jnp.where(high > 0.5, (high - 1.0) * 128.0 + low, float(ROWS_DEV))
    ids_ref[...] = value.astype(jnp.int32)


def order_kernel(capacity, group, ids_ref, pick_ref, sorted_ref, count_ref):
    devices = ids_ref.shape[0]
    slots = devices * capacity
    chunks = slots // LANES
    ids = ids_ref[...].astype(jnp.float32)
    lane = iota((1, LANES), 1)
    rolled = {}
    rows = [jnp.zeros((1, LANES), jnp.float32) for _ in range(chunks)]
    for s in range(devices):
        at, off = divmod(s * capacity, LANES)
        if off not in rolled:
            rolled[off] = pltpu.roll(ids, off, 1) if off else ids
        piece = rolled[off][s : s + 1, :]
        rows[at] = jnp.where((lane >= off) & (lane < off + capacity), piece, rows[at])
        if off + capacity > LANES:
            rows[at + 1] = jnp.where(lane < off + capacity - LANES, piece, rows[at + 1])
    edges = (lane * group).astype(jnp.float32)
    count = jnp.zeros((1, LANES), jnp.float32)
    ranks = [jnp.zeros((1, LANES), jnp.float32) for _ in range(chunks)]
    earlier = iota((LANES, LANES), 0) < iota((LANES, LANES), 1)
    for j in range(chunks):
        col = column(rows[j])
        count = count + jnp.sum(jnp.where(col < edges, 1.0, 0.0), axis=0, keepdims=True)
        for i in range(chunks):
            if j < i:
                hit = col <= rows[i]
            elif j > i:
                hit = col < rows[i]
            else:
                hit = (col < rows[i]) | ((col == rows[i]) & earlier)
            ranks[i] = ranks[i] + jnp.sum(jnp.where(hit, 1.0, 0.0), axis=0, keepdims=True)
    count_ref[...] = count.astype(jnp.int32)
    rank = jnp.concatenate(ranks, axis=1)
    row = jnp.concatenate(rows, axis=1).astype(jnp.int32)
    high = jnp.broadcast_to(lax.shift_right_logical(row, 7).astype(jnp.float32), (8, slots)).astype(jnp.bfloat16)
    low = jnp.broadcast_to((row & 127).astype(jnp.float32), (8, slots)).astype(jnp.bfloat16)
    for c in range(chunks):
        here = iota((LANES, slots), 0, jnp.float32) + float(c * LANES)
        pick = jnp.where(here == rank, 1.0, 0.0).astype(jnp.bfloat16)
        pick_ref[c * LANES : (c + 1) * LANES, :] = pick
        up = lax.dot_general(high, pick, NT, preferred_element_type=jnp.float32)
        down = lax.dot_general(low, pick, NT, preferred_element_type=jnp.float32)
        sorted_ref[c : c + 1, :] = (up * 128.0 + down)[0:1, :]


def stats_kernel(scale, blocks, *refs):
    q_ref = refs[0]
    k_refs = refs[1 : 1 + blocks]
    old = refs[1 + blocks : -2]
    top_ref, total_ref = refs[-2:]
    scores = [
        scale * lax.dot_general(k[...], q_ref[...], NT, preferred_element_type=jnp.float32) for k in k_refs
    ]
    top = functools.reduce(jnp.maximum, [jnp.max(s, axis=0, keepdims=True) for s in scores])
    if old:
        top = jnp.maximum(top, old[0][...])
    total = sum(jnp.sum(jnp.exp(s - top), axis=0, keepdims=True) for s in scores)
    if old:
        total = total + old[1][...] * jnp.exp(old[0][...] - top)
        top_ref[...] = top + jnp.log(total)
    else:
        top_ref[...] = top
    total_ref[...] = total


def query_kernel(scale, blocks, q_ref, lse_ref, pos_ref, *refs):
    k_refs, out_ref = refs[:blocks], refs[-1]
    size = q_ref.shape[0]
    total = None
    for m, k in enumerate(k_refs):
        scores = scale * lax.dot_general(k[...], q_ref[...], NT, preferred_element_type=jnp.float32)
        weights = jnp.exp(scores - lse_ref[...])
        if m == 0:
            weights = weights - jnp.where(iota((size, size), 0) == pos_ref[...], 1.0, 0.0)
        part = lax.dot_general(weights.astype(jnp.bfloat16), k[...], TN, preferred_element_type=jnp.float32)
        total = part if total is None else total + part
    out_ref[...] = (scale * total).astype(jnp.bfloat16)


def item_kernel(scale, blocks, k_ref, pick_ref, pos_ref, *refs):
    q_refs, lse_refs = refs[:blocks], refs[blocks : 2 * blocks]
    out_ref, send_ref = refs[-2:]
    size = k_ref.shape[0]
    part = 128

    def one(c, carry):
        at = pl.multiple_of(c * part, part)
        keys = k_ref[pl.ds(at, part), :]
        total = jnp.zeros((part, k_ref.shape[1]), jnp.float32)
        for m in range(blocks):
            scores = scale * lax.dot_general(keys, q_refs[m][...], NT, preferred_element_type=jnp.float32)
            weights = jnp.exp(scores - lse_refs[m][...])
            if m == 0:
                weights = weights - jnp.where(iota((part, size), 0) + at == pos_ref[...], 1.0, 0.0)
            total = total + jnp.dot(weights.astype(jnp.bfloat16), q_refs[m][...], preferred_element_type=jnp.float32)
        out_ref[pl.ds(at, part), :] = (scale * total).astype(jnp.bfloat16)
        return carry

    lax.fori_loop(0, size // part, one, 0)

    def two(c, carry):
        at = pl.multiple_of(c * SUB, SUB)
        send_ref[pl.ds(at, SUB), :] = jnp.dot(
            pick_ref[pl.ds(at, SUB), :], out_ref[...], preferred_element_type=jnp.float32
        ).astype(jnp.bfloat16)
        return carry

    lax.fori_loop(0, send_ref.shape[0] // SUB, two, 0)


def table_kernel(groups, count_ref, rows_ref, pick_ref, sorted_ref, out_ref, arranged, total):
    step = pl.program_id(0)
    chunks = arranged.shape[0] // LANES
    width = rows_ref.shape[1]

    @pl.when(step == 0)
    def _():
        used = (count_ref[pl.num_programs(0) * groups] + LANES - 1) // LANES

        def arrange(c, carry):
            at = pl.multiple_of(c * LANES, LANES)
            arranged[pl.ds(at, LANES), :] = jnp.dot(
                pick_ref[pl.ds(at, LANES), :], rows_ref[...], preferred_element_type=jnp.float32
            ).astype(jnp.bfloat16)
            return carry

        arranged[...] = jnp.zeros_like(arranged)
        lax.fori_loop(0, used, arrange, 0)

    def spread(chunk, base):
        at = pl.multiple_of(chunk * LANES, LANES)
        ids = jnp.concatenate([sorted_ref[pl.ds(chunk, 1), :], sorted_ref[pl.ds(chunk + 1, 1), :]], axis=1)
        local = ids - base.astype(jnp.float32)
        hot = jnp.where(iota((SUB, 2 * LANES), 0, jnp.float32) == local, 1.0, 0.0).astype(jnp.bfloat16)
        return jnp.dot(hot, arranged[pl.ds(at, 2 * LANES), :], preferred_element_type=jnp.float32)

    def group(g, carry):
        number = step * groups + g
        base = number * SUB
        at = pl.multiple_of(g * SUB, SUB)
        first = jnp.minimum(count_ref[number] // LANES, chunks - 2)
        out_ref[pl.ds(at, SUB), :] = spread(first, base).astype(jnp.bfloat16)
        end = count_ref[number + 1]

        @pl.when(end > (first + 2) * LANES)
        def _():
            total[...] = jnp.zeros((SUB, width), jnp.float32)

            def more(pair, inner):
                total[...] += spread(2 * pair, base)
                return inner

            lax.fori_loop(0, chunks // 2, more, 0)
            out_ref[pl.ds(at, SUB), :] = total[...].astype(jnp.bfloat16)

        return carry

    lax.fori_loop(0, groups, group, 0)


def local(queries, items, positives, item_owner, item_row):
    size, width = queries.shape
    scale = 3.0 / math.sqrt(width)
    blk_count = lax.axis_size("blk")
    window = blk_count // 2
    devices = blk_count * lax.axis_size("table")
    capacity = -(-(3 * size // devices) // 8) * 8
    slots = devices * capacity
    f32 = functools.partial(jax.ShapeDtypeStruct, dtype=jnp.float32)
    b16 = functools.partial(jax.ShapeDtypeStruct, dtype=jnp.bfloat16)
    i32 = functools.partial(jax.ShapeDtypeStruct, dtype=jnp.int32)

    owner_row = item_owner.reshape(1, size)
    row_row = item_row.reshape(1, size)
    pos_row = positives.reshape(1, size)

    twos = range(1, window // 2)
    k_two = [moved(items, "blk", lambda i, j=j: i + 2 * j) for j in twos]
    k_odd = moved(items, "blk", lambda i: i + window - 1 if i % 2 else i + 1)
    q_two = [moved(queries, "blk", lambda i, j=j: i - 2 * j) for j in twos]
    q_odd = moved(queries, "blk", lambda i: i - 1 if i % 2 else i - (window - 1))
    k_swap = [moved(k, "blk", lambda i: i ^ 1) for k in k_two]
    q_swap = [moved(q, "blk", lambda i: i ^ 1) for q in q_two]
    k_all = [k_odd, *k_two, *k_swap]
    q_all = [q_odd, *q_two, *q_swap]

    pick, ids = call(
        functools.partial(route_kernel, devices, capacity),
        (b16((slots, size)), i32((devices, LANES))),
        (owner_row, row_row),
        flops=4 * devices * LANES * size,
    )
    got_ids = lax.all_to_all(
        ids.reshape(devices, 1, LANES), ("blk", "table"), split_axis=0, concat_axis=0, tiled=True
    ).reshape(devices, LANES)
    table_groups = ROWS_DEV // SUB
    got_pick, got_sorted, got_count = call(
        functools.partial(order_kernel, capacity, SUB),
        (b16((slots, slots)), f32((slots // LANES, LANES)), i32((1, LANES))),
        (got_ids,),
        flops=32 * slots * slots,
    )

    pair = 2 * size * size * width
    top, total = call(
        functools.partial(stats_kernel, scale, 1),
        (f32((1, size)), f32((1, size))),
        (queries, items),
        flops=pair,
        trans=size * size,
    )
    lse, _ = call(
        functools.partial(stats_kernel, scale, len(k_all)),
        (f32((1, size)), f32((1, size))),
        (queries, *k_all, top, total),
        flops=pair * len(k_all),
        trans=size * size * len(k_all),
    )
    lse_odd = moved(lse, "blk", lambda i: i - 1 if i % 2 else i - (window - 1))
    lse_two = [moved(lse, "blk", lambda i, j=j: i - 2 * j) for j in twos]
    lse_swap = [moved(lse, "blk", lambda i, j=j: (i ^ 1) - 2 * j) for j in twos]
    lse_all = [lse_odd, *lse_two, *lse_swap]

    query_grad = call(
        functools.partial(query_kernel, scale, window),
        b16((size, width)),
        (queries, lse, pos_row, items, *k_all),
        flops=2 * pair * window,
        trans=size * size * window,
    )
    item_grad, send_rows = call(
        functools.partial(item_kernel, scale, window),
        (b16((size, width)), b16((slots, width))),
        (items, pick, pos_row, queries, *q_all, lse, *lse_all),
        flops=2 * pair * window + 2 * slots * size * width,
        trans=size * size * window,
    )
    got_rows = lax.all_to_all(
        send_rows.reshape(devices, capacity, width), ("blk", "table"), split_axis=0, concat_axis=0, tiled=True
    ).reshape(slots, width)
    groups = 8
    table_grad = pl.pallas_call(
        functools.partial(table_kernel, groups),
        out_shape=b16((ROWS_DEV, width)),
        grid_spec=pltpu.PrefetchScalarGridSpec(
            num_scalar_prefetch=1,
            grid=(table_groups // groups,),
            in_specs=[vmem(), vmem(), vmem()],
            out_specs=pl.BlockSpec((groups * SUB, width), lambda i, count: (i, 0)),
            scratch_shapes=[pltpu.VMEM((slots, width), jnp.bfloat16), pltpu.VMEM((SUB, width), jnp.float32)],
        ),
        cost_estimate=pl.CostEstimate(
            flops=2 * slots * slots * width, bytes_accessed=2 * ROWS_DEV * width, transcendentals=0
        ),
    )(got_count.reshape(LANES), got_rows, got_pick, got_sorted)
    return (query_grad, item_grad, table_grad)


def solution(mesh):
    both = P(("blk", "table"), None)
    flat = P(("blk", "table"))
    return jax.shard_map(
        local, mesh=mesh, in_specs=(both, both, flat, both, flat), out_specs=(both, both, both), check_vma=False
    )
```

```python
import functools
import math

import jax
import jax.numpy as jnp
from jax import lax
from jax.experimental import pallas as pl
from jax.experimental.pallas import tpu as pltpu
from jax.sharding import PartitionSpec as P


ROWS_DEV = 16384
LANES = 128
SUB = 256
LOG2E = math.log2(math.e)
NT = (((1,), (1,)), ((), ()))
TN = (((0,), (0,)), ((), ()))


def moved(block, axis, target_of):
    count = lax.axis_size(axis)
    return lax.ppermute(block, axis, [(i, target_of(i) % count) for i in range(count)])


def vmem():
    return pl.BlockSpec(memory_space=pltpu.VMEM)


def params(mib):
    return pltpu.CompilerParams(vmem_limit_bytes=mib * 2**20)


def call(body, out_shape, args, flops=0, trans=0, mib=12):
    moved_bytes = sum(a.size * a.dtype.itemsize for a in args)
    outs = out_shape if isinstance(out_shape, (tuple, list)) else (out_shape,)
    moved_bytes += sum(math.prod(o.shape) * o.dtype.itemsize for o in outs)
    specs = [vmem() for _ in outs]
    return pl.pallas_call(
        body,
        out_shape=out_shape,
        in_specs=[vmem() for _ in args],
        out_specs=specs if isinstance(out_shape, (tuple, list)) else specs[0],
        cost_estimate=pl.CostEstimate(flops=flops, bytes_accessed=moved_bytes, transcendentals=trans),
        compiler_params=params(mib),
    )(*args)


def iota(shape, dim, dtype=jnp.int32):
    value = lax.broadcasted_iota(jnp.int32, shape, dim)
    return value if dtype == jnp.int32 else value.astype(dtype)


def column(row):
    wide = jnp.broadcast_to(row, (LANES, LANES))
    return jnp.transpose(wide)


def one_hot(shape, row, base):
    there = (iota(shape, 0) + base).astype(jnp.int16)
    return jnp.where(there == row.astype(jnp.int16), jnp.bfloat16(1), jnp.bfloat16(0))


def route_kernel(devices, capacity, owner_ref, row_ref, slot_ref, ids_ref):
    size = owner_ref.shape[1]
    owner = owner_ref[...]
    rank = jnp.zeros((1, size), jnp.float32)
    for base in range(0, size, LANES):
        col = column(owner[:, base : base + LANES])
        col = jnp.concatenate([col] * (size // LANES), axis=1)
        here = iota((LANES, size), 0) + base
        hit = (col == owner) & (here < iota((LANES, size), 1))
        rank = rank + jnp.sum(jnp.where(hit, 1.0, 0.0), axis=0, keepdims=True)
    rank = rank.astype(jnp.int32)
    slot_ref[...] = owner * capacity + rank
    row = row_ref[...]
    high = (lax.shift_right_logical(row, 7) + 1).astype(jnp.float32)
    low = (row & 127).astype(jnp.float32)
    mine = iota((devices, size), 0) == owner
    place = one_hot((LANES, size), rank, 0)
    high = jnp.where(mine, high, 0.0).astype(jnp.bfloat16)
    low = jnp.where(mine, low, 0.0).astype(jnp.bfloat16)
    high = lax.dot_general(high, place, NT, preferred_element_type=jnp.float32)
    low = lax.dot_general(low, place, NT, preferred_element_type=jnp.float32)
    value = jnp.where(high > 0.5, (high - 1.0) * 128.0 + low, float(ROWS_DEV))
    ids_ref[...] = value.astype(jnp.int32)


def order_kernel(capacity, group, ids_ref, rank_ref, sorted_ref, count_ref):
    devices = ids_ref.shape[0]
    slots = devices * capacity
    chunks = slots // LANES
    ids = ids_ref[...]
    lane = iota((1, LANES), 1)
    rolled = {}
    rows = [jnp.zeros((1, LANES), jnp.int32) for _ in range(chunks)]
    for s in range(devices):
        at, off = divmod(s * capacity, LANES)
        if off not in rolled:
            rolled[off] = pltpu.roll(ids, off, 1) if off else ids
        piece = rolled[off][s : s + 1, :]
        rows[at] = jnp.where((lane >= off) & (lane < off + capacity), piece, rows[at])
        if off + capacity > LANES:
            rows[at + 1] = jnp.where(lane < off + capacity - LANES, piece, rows[at + 1])
    edges = lane * group
    count = jnp.zeros((1, LANES), jnp.float32)
    ranks = [jnp.zeros((1, LANES), jnp.float32) for _ in range(chunks)]
    earlier = iota((LANES, LANES), 0) < iota((LANES, LANES), 1)
    for j in range(chunks):
        col = column(rows[j])
        count = count + jnp.sum(jnp.where(col < edges, 1.0, 0.0), axis=0, keepdims=True)
        for i in range(chunks):
            if j < i:
                hit = col <= rows[i]
            elif j > i:
                hit = col < rows[i]
            else:
                hit = (col < rows[i]) | ((col == rows[i]) & earlier)
            ranks[i] = ranks[i] + jnp.sum(jnp.where(hit, 1.0, 0.0), axis=0, keepdims=True)
    count_ref[...] = count.astype(jnp.int32)
    rank = jnp.concatenate(ranks, axis=1).astype(jnp.int32)
    rank_ref[...] = rank
    row = jnp.concatenate(rows, axis=1)
    high = jnp.broadcast_to(lax.shift_right_logical(row, 7).astype(jnp.float32), (8, slots)).astype(jnp.bfloat16)
    low = jnp.broadcast_to((row & 127).astype(jnp.float32), (8, slots)).astype(jnp.bfloat16)
    for c in range(chunks):
        pick = one_hot((LANES, slots), rank, c * LANES)
        up = lax.dot_general(high, pick, NT, preferred_element_type=jnp.float32)
        down = lax.dot_general(low, pick, NT, preferred_element_type=jnp.float32)
        sorted_ref[c : c + 1, :] = (up * 128.0 + down)[0:1, :].astype(jnp.int32)


def stats_kernel(scale, blocks, olds, *refs):
    q_ref = refs[0]
    k_refs = refs[1 : 1 + blocks]
    old = refs[1 + blocks : 1 + blocks + olds]
    top_ref, total_ref = refs[-2:]
    size = q_ref.shape[0]
    for base in range(0, size, SUB):
        q = q_ref[base : base + SUB, :]
        at = slice(base, base + SUB)
        top = old[0][:, at] if old else None
        total = old[1][:, at] if old else None
        for k in k_refs:
            scores = scale * lax.dot_general(k[...], q, NT, preferred_element_type=jnp.float32)
            high = jnp.max(scores, axis=0, keepdims=True)
            high = high if top is None else jnp.maximum(top, high)
            part = jnp.sum(jnp.exp2(scores - high), axis=0, keepdims=True)
            total = part if top is None else total * jnp.exp2(top - high) + part
            top = high
        top_ref[:, at] = top + jnp.log2(total) if old else top
        total_ref[:, at] = total


def query_kernel(scale, blocks, q_ref, lse_ref, pos_ref, *refs):
    k_refs, out_ref = refs[:blocks], refs[-1]
    size = q_ref.shape[0]
    for base in range(0, size, SUB):
        at = slice(base, base + SUB)
        q = q_ref[at, :]
        total = None
        for m, k in enumerate(k_refs):
            scores = (scale * LOG2E) * lax.dot_general(k[...], q, NT, preferred_element_type=jnp.float32)
            weights = jnp.exp2(scores - lse_ref[:, at])
            if m == 0:
                weights = weights - jnp.where(iota((size, SUB), 0) == pos_ref[:, at], 1.0, 0.0)
            part = lax.dot_general(weights.astype(jnp.bfloat16), k[...], TN, preferred_element_type=jnp.float32)
            total = part if total is None else total + part
        out_ref[at, :] = (scale * total).astype(jnp.bfloat16)


def item_kernel(scale, blocks, k_ref, slot_ref, pos_ref, *refs):
    q_refs, lse_refs = refs[:blocks], refs[blocks : 2 * blocks]
    out_ref, send_ref = refs[-2:]
    size = k_ref.shape[0]
    keys = k_ref[...]
    total = None
    for m in range(blocks):
        for base in range(0, size, SUB):
            at = slice(base, base + SUB)
            q = q_refs[m][at, :]
            scores = (scale * LOG2E) * lax.dot_general(keys, q, NT, preferred_element_type=jnp.float32)
            weights = jnp.exp2(scores - lse_refs[m][:, at])
            if m == 0:
                weights = weights - jnp.where(iota((size, SUB), 0) == pos_ref[:, at], 1.0, 0.0)
            part = jnp.dot(weights.astype(jnp.bfloat16), q, preferred_element_type=jnp.float32)
            total = part if total is None else total + part
    grad = (scale * total).astype(jnp.bfloat16)
    out_ref[...] = grad
    for base in range(0, send_ref.shape[0], SUB):
        pick = one_hot((SUB, size), slot_ref[...], base)
        part = jnp.dot(pick, grad, preferred_element_type=jnp.float32)
        send_ref[base : base + SUB, :] = part.astype(jnp.bfloat16)


def table_kernel(groups, count_ref, rows_ref, rank_ref, sorted_ref, out_ref, pick, arranged, total):
    step = pl.program_id(0)
    chunks = arranged.shape[0] // LANES
    width = rows_ref.shape[1]

    @pl.when(step == 0)
    def _():
        for at in range(0, chunks * LANES, SUB):
            pick[at : at + SUB, :] = one_hot((SUB, chunks * LANES), rank_ref[...], at)
        arranged[...] = jnp.dot(pick[...], rows_ref[...], preferred_element_type=jnp.float32).astype(jnp.bfloat16)

    def spread(chunk, base):
        at = pl.multiple_of(chunk * LANES, LANES)
        ids = jnp.concatenate([sorted_ref[pl.ds(chunk, 1), :], sorted_ref[pl.ds(chunk + 1, 1), :]], axis=1)
        hot = one_hot((SUB, 2 * LANES), ids - base, 0)
        return jnp.dot(hot, arranged[pl.ds(at, 2 * LANES), :], preferred_element_type=jnp.float32)

    firsts = [jnp.minimum(count_ref[step * groups + g] // LANES, chunks - 2) for g in range(groups)]
    overs = [count_ref[step * groups + g + 1] > (firsts[g] + 2) * LANES for g in range(groups)]
    for g in range(groups):
        out_ref[g * SUB : (g + 1) * SUB, :] = spread(firsts[g], (step * groups + g) * SUB).astype(jnp.bfloat16)

    @pl.when(functools.reduce(jnp.logical_or, overs))
    def _():
        def group(g, carry):
            base = (step * groups + g) * SUB
            total[...] = jnp.zeros((SUB, width), jnp.float32)

            def more(pair, inner):
                total[...] += spread(2 * pair, base)
                return inner

            lax.fori_loop(0, chunks // 2, more, 0)
            out_ref[pl.ds(pl.multiple_of(g * SUB, SUB), SUB), :] = total[...].astype(jnp.bfloat16)
            return carry

        lax.fori_loop(0, groups, group, 0)


def local(queries, items, positives, item_owner, item_row):
    size, width = queries.shape
    scale = 3.0 / math.sqrt(width)
    blk_count = lax.axis_size("blk")
    window = blk_count // 2
    devices = blk_count * lax.axis_size("table")
    capacity = -(-(3 * size // devices) // 8) * 8
    slots = devices * capacity
    f32 = functools.partial(jax.ShapeDtypeStruct, dtype=jnp.float32)
    b16 = functools.partial(jax.ShapeDtypeStruct, dtype=jnp.bfloat16)
    i32 = functools.partial(jax.ShapeDtypeStruct, dtype=jnp.int32)

    owner_row = item_owner.reshape(1, size)
    row_row = item_row.reshape(1, size)
    pos_row = positives.reshape(1, size)

    pair = 2 * size * size * width
    twos = range(1, window // 2)
    k_two = [moved(items, "blk", lambda i, j=j: i + 2 * j) for j in twos]
    k_odd = moved(items, "blk", lambda i: i + window - 1 if i % 2 else i + 1)
    q_two = [moved(queries, "blk", lambda i, j=j: i - 2 * j) for j in twos]
    q_odd = moved(queries, "blk", lambda i: i - 1 if i % 2 else i - (window - 1))
    slot, ids = call(
        functools.partial(route_kernel, devices, capacity),
        (i32((1, size)), i32((devices, LANES))),
        (owner_row, row_row),
        flops=4 * devices * LANES * size,
    )
    got_ids = lax.all_to_all(
        ids.reshape(devices, 1, LANES), ("blk", "table"), split_axis=0, concat_axis=0, tiled=True
    ).reshape(devices, LANES)
    top, total = call(
        functools.partial(stats_kernel, scale * LOG2E, 1, 0),
        (f32((1, size)), f32((1, size))),
        (queries, items),
        flops=pair,
        trans=size * size,
    )
    k_two, q_two, got_ids = lax.optimization_barrier((k_two, q_two, got_ids))
    k_swap = [moved(k, "blk", lambda i: i ^ 1) for k in k_two]
    q_swap = [moved(q, "blk", lambda i: i ^ 1) for q in q_two]
    k_all = [k_odd, *k_two, *k_swap]
    q_all = [q_odd, *q_two, *q_swap]
    table_groups = ROWS_DEV // SUB
    lse, _ = call(
        functools.partial(stats_kernel, scale * LOG2E, len(k_all), 2),
        (f32((1, size)), f32((1, size))),
        (queries, *k_all, top, total),
        flops=pair * len(k_all),
        trans=size * size * len(k_all),
    )
    got_rank, got_sorted, got_count = call(
        functools.partial(order_kernel, capacity, SUB),
        (i32((1, slots)), i32((slots // LANES, LANES)), i32((1, LANES))),
        (got_ids,),
        flops=32 * slots * slots,
    )
    lse_odd = moved(lse, "blk", lambda i: i - 1 if i % 2 else i - (window - 1))
    lse_two = [moved(lse, "blk", lambda i, j=j: i - 2 * j) for j in twos]
    lse_swap = [moved(lse, "blk", lambda i, j=j: (i ^ 1) - 2 * j) for j in twos]
    lse_all = [lse_odd, *lse_two, *lse_swap]

    query_grad = call(
        functools.partial(query_kernel, scale, window),
        b16((size, width)),
        (queries, lse, pos_row, items, *k_all),
        flops=2 * pair * window,
        trans=size * size * window,
    )
    item_grad, send_rows = call(
        functools.partial(item_kernel, scale, window),
        (b16((size, width)), b16((slots, width))),
        (items, slot, pos_row, queries, *q_all, lse, *lse_all),
        flops=2 * pair * window + 2 * slots * size * width,
        trans=size * size * window,
    )
    got_rows = lax.all_to_all(
        send_rows.reshape(devices, capacity, width), ("blk", "table"), split_axis=0, concat_axis=0, tiled=True
    ).reshape(slots, width)
    groups = 8
    table_grad = pl.pallas_call(
        functools.partial(table_kernel, groups),
        out_shape=b16((ROWS_DEV, width)),
        grid_spec=pltpu.PrefetchScalarGridSpec(
            num_scalar_prefetch=1,
            grid=(table_groups // groups,),
            in_specs=[vmem(), vmem(), vmem()],
            out_specs=pl.BlockSpec((groups * SUB, width), lambda i, count: (i, 0)),
            scratch_shapes=[pltpu.VMEM((slots, slots), jnp.bfloat16), pltpu.VMEM((slots, width), jnp.bfloat16), pltpu.VMEM((SUB, width), jnp.float32)],
        ),
        compiler_params=params(24),
        cost_estimate=pl.CostEstimate(
            flops=2 * slots * slots * width, bytes_accessed=2 * ROWS_DEV * width, transcendentals=0
        ),
    )(got_count.reshape(LANES), got_rows, got_rank, got_sorted)
    return (query_grad, item_grad, table_grad)


def solution(mesh):
    both = P(("blk", "table"), None)
    flat = P(("blk", "table"))
    return jax.shard_map(
        local, mesh=mesh, in_specs=(both, both, flat, both, flat), out_specs=(both, both, both), check_vma=False
    )
```

```python
import functools
import math

import jax
import jax.numpy as jnp
from jax import lax
from jax.experimental import pallas as pl
from jax.experimental.pallas import tpu as pltpu
from jax.sharding import PartitionSpec as P


ROWS_DEV = 16384
LANES = 128
SUB = 256
LOG2E = math.log2(math.e)
NT = (((1,), (1,)), ((), ()))
TN = (((0,), (0,)), ((), ()))


def moved(block, axis, target_of):
    count = lax.axis_size(axis)
    return lax.ppermute(block, axis, [(i, target_of(i) % count) for i in range(count)])


def vmem():
    return pl.BlockSpec(memory_space=pltpu.VMEM)


def params(mib):
    return pltpu.CompilerParams(vmem_limit_bytes=mib * 2**20)


def call(body, out_shape, args, flops=0, trans=0, mib=12):
    moved_bytes = sum(a.size * a.dtype.itemsize for a in args)
    outs = out_shape if isinstance(out_shape, (tuple, list)) else (out_shape,)
    moved_bytes += sum(math.prod(o.shape) * o.dtype.itemsize for o in outs)
    specs = [vmem() for _ in outs]
    return pl.pallas_call(
        body,
        out_shape=out_shape,
        in_specs=[vmem() for _ in args],
        out_specs=specs if isinstance(out_shape, (tuple, list)) else specs[0],
        cost_estimate=pl.CostEstimate(flops=flops, bytes_accessed=moved_bytes, transcendentals=trans),
        compiler_params=params(mib),
    )(*args)


def iota(shape, dim, dtype=jnp.int32):
    value = lax.broadcasted_iota(jnp.int32, shape, dim)
    return value if dtype == jnp.int32 else value.astype(dtype)


def column(row):
    wide = jnp.broadcast_to(row, (LANES, LANES))
    return jnp.transpose(wide)


def one_hot(shape, row, base):
    there = (iota(shape, 0) + base).astype(jnp.int16)
    return jnp.where(there == row.astype(jnp.int16), jnp.bfloat16(1), jnp.bfloat16(0))


def first_kernel(scale, devices, capacity, *refs):
    sources, results, (owner_ref, row_ref, done) = refs[:5], refs[5:12], refs[12:]
    slot_ref, ids_ref, top_ref, total_ref, pos_ref, q_ref, k_ref = results
    targets = (owner_ref, row_ref, k_ref, q_ref, pos_ref)
    copies = [pltpu.make_async_copy(a, b, done.at[i]) for i, (a, b) in enumerate(zip(sources, targets))]
    for copy in copies:
        copy.start()
    copies[0].wait()
    copies[1].wait()
    route(devices, capacity, owner_ref, row_ref, slot_ref, ids_ref)
    copies[2].wait()
    copies[3].wait()
    stats_kernel(scale, 1, 0, q_ref, k_ref, top_ref, total_ref)
    copies[4].wait()


def route(devices, capacity, owner_ref, row_ref, slot_ref, ids_ref):
    size = owner_ref.shape[1]
    owner = owner_ref[...]
    rank = jnp.zeros((1, size), jnp.float32)
    for base in range(0, size, LANES):
        col = column(owner[:, base : base + LANES])
        col = jnp.concatenate([col] * (size // LANES), axis=1)
        here = iota((LANES, size), 0) + base
        hit = (col == owner) & (here < iota((LANES, size), 1))
        rank = rank + jnp.sum(jnp.where(hit, 1.0, 0.0), axis=0, keepdims=True)
    rank = rank.astype(jnp.int32)
    slot_ref[...] = owner * capacity + rank
    row = row_ref[...]
    high = (lax.shift_right_logical(row, 7) + 1).astype(jnp.float32)
    low = (row & 127).astype(jnp.float32)
    mine = iota((devices, size), 0) == owner
    place = one_hot((LANES, size), rank, 0)
    high = jnp.where(mine, high, 0.0).astype(jnp.bfloat16)
    low = jnp.where(mine, low, 0.0).astype(jnp.bfloat16)
    high = lax.dot_general(high, place, NT, preferred_element_type=jnp.float32)
    low = lax.dot_general(low, place, NT, preferred_element_type=jnp.float32)
    value = jnp.where(high > 0.5, (high - 1.0) * 128.0 + low, float(ROWS_DEV))
    ids_ref[...] = value.astype(jnp.int32)


def order_kernel(capacity, group, ids_ref, rank_ref, sorted_ref, count_ref):
    devices = ids_ref.shape[0]
    slots = devices * capacity
    chunks = slots // LANES
    ids = ids_ref[...]
    lane = iota((1, LANES), 1)
    rolled = {}
    rows = [jnp.zeros((1, LANES), jnp.int32) for _ in range(chunks)]
    for s in range(devices):
        at, off = divmod(s * capacity, LANES)
        if off not in rolled:
            rolled[off] = pltpu.roll(ids, off, 1) if off else ids
        piece = rolled[off][s : s + 1, :]
        rows[at] = jnp.where((lane >= off) & (lane < off + capacity), piece, rows[at])
        if off + capacity > LANES:
            rows[at + 1] = jnp.where(lane < off + capacity - LANES, piece, rows[at + 1])
    edges = lane * group
    count = jnp.zeros((1, LANES), jnp.float32)
    ranks = [jnp.zeros((1, LANES), jnp.float32) for _ in range(chunks)]
    earlier = iota((LANES, LANES), 0) < iota((LANES, LANES), 1)
    for j in range(chunks):
        col = column(rows[j])
        count = count + jnp.sum(jnp.where(col < edges, 1.0, 0.0), axis=0, keepdims=True)
        for i in range(chunks):
            if j < i:
                hit = col <= rows[i]
            elif j > i:
                hit = col < rows[i]
            else:
                hit = (col < rows[i]) | ((col == rows[i]) & earlier)
            ranks[i] = ranks[i] + jnp.sum(jnp.where(hit, 1.0, 0.0), axis=0, keepdims=True)
    count_ref[...] = count.astype(jnp.int32)
    rank = jnp.concatenate(ranks, axis=1).astype(jnp.int32)
    rank_ref[...] = rank
    row = jnp.concatenate(rows, axis=1)
    high = jnp.broadcast_to(lax.shift_right_logical(row, 7).astype(jnp.float32), (8, slots)).astype(jnp.bfloat16)
    low = jnp.broadcast_to((row & 127).astype(jnp.float32), (8, slots)).astype(jnp.bfloat16)
    for c in range(chunks):
        pick = one_hot((LANES, slots), rank, c * LANES)
        up = lax.dot_general(high, pick, NT, preferred_element_type=jnp.float32)
        down = lax.dot_general(low, pick, NT, preferred_element_type=jnp.float32)
        sorted_ref[c : c + 1, :] = (up * 128.0 + down)[0:1, :].astype(jnp.int32)


def stats_kernel(scale, blocks, olds, *refs):
    q_ref = refs[0]
    k_refs = refs[1 : 1 + blocks]
    old = refs[1 + blocks : 1 + blocks + olds]
    top_ref, total_ref = refs[-2:]
    size = q_ref.shape[0]
    for base in range(0, size, SUB):
        q = q_ref[base : base + SUB, :]
        at = slice(base, base + SUB)
        top = old[0][:, at] if old else None
        total = old[1][:, at] if old else None
        for k in k_refs:
            scores = scale * lax.dot_general(k[...], q, NT, preferred_element_type=jnp.float32)
            high = jnp.max(scores, axis=0, keepdims=True)
            high = high if top is None else jnp.maximum(top, high)
            part = jnp.sum(jnp.exp2(scores - high), axis=0, keepdims=True)
            total = part if top is None else total * jnp.exp2(top - high) + part
            top = high
        top_ref[:, at] = top + jnp.log2(total) if old else top
        total_ref[:, at] = total


def query_kernel(scale, blocks, q_ref, lse_ref, pos_ref, *refs):
    k_refs, out_ref = refs[:blocks], refs[-1]
    size = q_ref.shape[0]
    for base in range(0, size, SUB):
        at = slice(base, base + SUB)
        q = q_ref[at, :]
        total = None
        for m, k in enumerate(k_refs):
            scores = (scale * LOG2E) * lax.dot_general(k[...], q, NT, preferred_element_type=jnp.float32)
            weights = jnp.exp2(scores - lse_ref[:, at])
            if m == 0:
                weights = weights - jnp.where(iota((size, SUB), 0) == pos_ref[:, at], 1.0, 0.0)
            part = lax.dot_general(weights.astype(jnp.bfloat16), k[...], TN, preferred_element_type=jnp.float32)
            total = part if total is None else total + part
        out_ref[at, :] = (scale * total).astype(jnp.bfloat16)


def item_kernel(scale, blocks, k_ref, slot_ref, pos_ref, *refs):
    q_refs, lse_refs = refs[:blocks], refs[blocks : 2 * blocks]
    out_ref, send_ref = refs[-2:]
    size = k_ref.shape[0]
    keys = k_ref[...]
    total = None
    for m in range(blocks):
        for base in range(0, size, SUB):
            at = slice(base, base + SUB)
            q = q_refs[m][at, :]
            scores = (scale * LOG2E) * lax.dot_general(keys, q, NT, preferred_element_type=jnp.float32)
            weights = jnp.exp2(scores - lse_refs[m][:, at])
            if m == 0:
                weights = weights - jnp.where(iota((size, SUB), 0) == pos_ref[:, at], 1.0, 0.0)
            part = jnp.dot(weights.astype(jnp.bfloat16), q, preferred_element_type=jnp.float32)
            total = part if total is None else total + part
    grad = (scale * total).astype(jnp.bfloat16)
    out_ref[...] = grad
    for base in range(0, send_ref.shape[0], SUB):
        pick = one_hot((SUB, size), slot_ref[...], base)
        part = jnp.dot(pick, grad, preferred_element_type=jnp.float32)
        send_ref[base : base + SUB, :] = part.astype(jnp.bfloat16)


def table_kernel(groups, count_ref, rows_ref, rank_ref, sorted_ref, out_ref, pick, arranged, total):
    step = pl.program_id(0)
    chunks = arranged.shape[0] // LANES
    width = rows_ref.shape[1]

    @pl.when(step == 0)
    def _():
        for at in range(0, chunks * LANES, SUB):
            pick[at : at + SUB, :] = one_hot((SUB, chunks * LANES), rank_ref[...], at)
        arranged[...] = jnp.dot(pick[...], rows_ref[...], preferred_element_type=jnp.float32).astype(jnp.bfloat16)

    def spread(chunk, base):
        at = pl.multiple_of(chunk * LANES, LANES)
        ids = jnp.concatenate([sorted_ref[pl.ds(chunk, 1), :], sorted_ref[pl.ds(chunk + 1, 1), :]], axis=1)
        hot = one_hot((SUB, 2 * LANES), ids - base, 0)
        return jnp.dot(hot, arranged[pl.ds(at, 2 * LANES), :], preferred_element_type=jnp.float32)

    firsts = [jnp.minimum(count_ref[step * groups + g] // LANES, chunks - 2) for g in range(groups)]
    overs = [count_ref[step * groups + g + 1] > (firsts[g] + 2) * LANES for g in range(groups)]
    for g in range(groups):
        out_ref[g * SUB : (g + 1) * SUB, :] = spread(firsts[g], (step * groups + g) * SUB).astype(jnp.bfloat16)

    @pl.when(functools.reduce(jnp.logical_or, overs))
    def _():
        def group(g, carry):
            base = (step * groups + g) * SUB
            total[...] = jnp.zeros((SUB, width), jnp.float32)

            def more(pair, inner):
                total[...] += spread(2 * pair, base)
                return inner

            lax.fori_loop(0, chunks // 2, more, 0)
            out_ref[pl.ds(pl.multiple_of(g * SUB, SUB), SUB), :] = total[...].astype(jnp.bfloat16)
            return carry

        lax.fori_loop(0, groups, group, 0)


def local(queries, items, positives, item_owner, item_row):
    size, width = queries.shape
    scale = 3.0 / math.sqrt(width)
    blk_count = lax.axis_size("blk")
    window = blk_count // 2
    devices = blk_count * lax.axis_size("table")
    capacity = -(-(3 * size // devices) // 8) * 8
    slots = devices * capacity
    f32 = functools.partial(jax.ShapeDtypeStruct, dtype=jnp.float32)
    b16 = functools.partial(jax.ShapeDtypeStruct, dtype=jnp.bfloat16)
    i32 = functools.partial(jax.ShapeDtypeStruct, dtype=jnp.int32)

    owner_row = item_owner.reshape(1, size)
    row_row = item_row.reshape(1, size)
    pos_row = positives.reshape(1, size)

    pair = 2 * size * size * width
    twos = range(1, window // 2)
    k_two = [moved(items, "blk", lambda i, j=j: i + 2 * j) for j in twos]
    k_odd = moved(items, "blk", lambda i: i + window - 1 if i % 2 else i + 1)
    q_two = [moved(queries, "blk", lambda i, j=j: i - 2 * j) for j in twos]
    q_odd = moved(queries, "blk", lambda i: i - 1 if i % 2 else i - (window - 1))
    slot, ids, top, total, pos_row, queries, items = pl.pallas_call(
        functools.partial(first_kernel, scale * LOG2E, devices, capacity),
        out_shape=(
            i32((1, size)),
            i32((devices, LANES)),
            f32((1, size)),
            f32((1, size)),
            i32((1, size)),
            b16((size, width)),
            b16((size, width)),
        ),
        in_specs=[pl.BlockSpec(memory_space=pltpu.HBM) for _ in range(5)],
        out_specs=tuple(vmem() for _ in range(7)),
        scratch_shapes=[
            pltpu.VMEM((1, size), jnp.int32),
            pltpu.VMEM((1, size), jnp.int32),
            pltpu.SemaphoreType.DMA((5,)),
        ],
        compiler_params=params(12),
        cost_estimate=pl.CostEstimate(flops=pair, bytes_accessed=4 * size * width, transcendentals=size * size),
    )(*[pltpu.with_memory_space_constraint(x, pltpu.HBM) for x in (owner_row, row_row, items, queries, pos_row)])
    got_ids = lax.all_to_all(
        ids.reshape(devices, 1, LANES), ("blk", "table"), split_axis=0, concat_axis=0, tiled=True
    ).reshape(devices, LANES)
    k_swap = [moved(k, "blk", lambda i: i ^ 1) for k in k_two]
    q_swap = [moved(q, "blk", lambda i: i ^ 1) for q in q_two]
    k_all = [k_odd, *k_two, *k_swap]
    q_all = [q_odd, *q_two, *q_swap]
    table_groups = ROWS_DEV // SUB
    lse, _ = call(
        functools.partial(stats_kernel, scale * LOG2E, len(k_all), 2),
        (f32((1, size)), f32((1, size))),
        (queries, *k_all, top, total),
        flops=pair * len(k_all),
        trans=size * size * len(k_all),
    )
    got_rank, got_sorted, got_count = call(
        functools.partial(order_kernel, capacity, SUB),
        (i32((1, slots)), i32((slots // LANES, LANES)), i32((1, LANES))),
        (got_ids,),
        flops=32 * slots * slots,
    )
    lse_odd = moved(lse, "blk", lambda i: i - 1 if i % 2 else i - (window - 1))
    lse_two = [moved(lse, "blk", lambda i, j=j: i - 2 * j) for j in twos]
    lse_swap = [moved(lse, "blk", lambda i, j=j: (i ^ 1) - 2 * j) for j in twos]
    lse_all = [lse_odd, *lse_two, *lse_swap]

    query_grad = call(
        functools.partial(query_kernel, scale, window),
        b16((size, width)),
        (queries, lse, pos_row, items, *k_all),
        flops=2 * pair * window,
        trans=size * size * window,
    )
    item_grad, send_rows = call(
        functools.partial(item_kernel, scale, window),
        (b16((size, width)), b16((slots, width))),
        (items, slot, pos_row, queries, *q_all, lse, *lse_all),
        flops=2 * pair * window + 2 * slots * size * width,
        trans=size * size * window,
    )
    got_rows = lax.all_to_all(
        send_rows.reshape(devices, capacity, width), ("blk", "table"), split_axis=0, concat_axis=0, tiled=True
    ).reshape(slots, width)
    groups = 8
    table_grad = pl.pallas_call(
        functools.partial(table_kernel, groups),
        out_shape=b16((ROWS_DEV, width)),
        grid_spec=pltpu.PrefetchScalarGridSpec(
            num_scalar_prefetch=1,
            grid=(table_groups // groups,),
            in_specs=[vmem(), vmem(), vmem()],
            out_specs=pl.BlockSpec((groups * SUB, width), lambda i, count: (i, 0)),
            scratch_shapes=[pltpu.VMEM((slots, slots), jnp.bfloat16), pltpu.VMEM((slots, width), jnp.bfloat16), pltpu.VMEM((SUB, width), jnp.float32)],
        ),
        compiler_params=params(24),
        cost_estimate=pl.CostEstimate(
            flops=2 * slots * slots * width, bytes_accessed=2 * ROWS_DEV * width, transcendentals=0
        ),
    )(got_count.reshape(LANES), got_rows, got_rank, got_sorted)
    return (query_grad, item_grad, table_grad)


def solution(mesh):
    both = P(("blk", "table"), None)
    flat = P(("blk", "table"))
    return jax.shard_map(
        local, mesh=mesh, in_specs=(both, both, flat, both, flat), out_specs=(both, both, both), check_vma=False
    )
```

```python
import functools
import math

import jax
import jax.numpy as jnp
from jax import lax
from jax.experimental import pallas as pl
from jax.experimental.pallas import tpu as pltpu
from jax.sharding import PartitionSpec as P


ROWS_DEV = 16384
LANES = 128
SUB = 256
LOG2E = math.log2(math.e)
NT = (((1,), (1,)), ((), ()))
TN = (((0,), (0,)), ((), ()))


def moved(block, axis, target_of):
    count = lax.axis_size(axis)
    return lax.ppermute(block, axis, [(i, target_of(i) % count) for i in range(count)])


def vmem():
    return pl.BlockSpec(memory_space=pltpu.VMEM)


def params(mib):
    return pltpu.CompilerParams(vmem_limit_bytes=mib * 2**20)


def call(body, out_shape, args, flops=0, trans=0, mib=12):
    moved_bytes = sum(a.size * a.dtype.itemsize for a in args)
    outs = out_shape if isinstance(out_shape, (tuple, list)) else (out_shape,)
    moved_bytes += sum(math.prod(o.shape) * o.dtype.itemsize for o in outs)
    specs = [vmem() for _ in outs]
    return pl.pallas_call(
        body,
        out_shape=out_shape,
        in_specs=[vmem() for _ in args],
        out_specs=specs if isinstance(out_shape, (tuple, list)) else specs[0],
        cost_estimate=pl.CostEstimate(flops=flops, bytes_accessed=moved_bytes, transcendentals=trans),
        compiler_params=params(mib),
    )(*args)


def iota(shape, dim, dtype=jnp.int32):
    value = lax.broadcasted_iota(jnp.int32, shape, dim)
    return value if dtype == jnp.int32 else value.astype(dtype)


def column(row):
    wide = jnp.broadcast_to(row, (LANES, LANES))
    return jnp.transpose(wide)


def one_hot(shape, row, base):
    there = (iota(shape, 0) + base).astype(jnp.int16)
    return jnp.where(there == row.astype(jnp.int16), jnp.bfloat16(1), jnp.bfloat16(0))


def first_kernel(scale, devices, capacity, *refs):
    sources, results, (owner_ref, row_ref, done) = refs[:5], refs[5:12], refs[12:]
    slot_ref, ids_ref, top_ref, total_ref, pos_ref, q_ref, k_ref = results
    targets = (owner_ref, row_ref, k_ref, q_ref, pos_ref)
    copies = [pltpu.make_async_copy(a, b, done.at[i]) for i, (a, b) in enumerate(zip(sources, targets))]
    for copy in copies:
        copy.start()
    copies[0].wait()
    copies[1].wait()
    route(devices, capacity, owner_ref, row_ref, slot_ref, ids_ref)
    copies[2].wait()
    copies[3].wait()
    stats_kernel(scale, 1, 0, False, q_ref, k_ref, top_ref, total_ref)
    copies[4].wait()


def route(devices, capacity, owner_ref, row_ref, slot_ref, ids_ref):
    size = owner_ref.shape[1]
    owner = owner_ref[...]
    rank = jnp.zeros((1, size), jnp.float32)
    for base in range(0, size, LANES):
        col = column(owner[:, base : base + LANES])
        col = jnp.concatenate([col] * (size // LANES), axis=1)
        here = iota((LANES, size), 0) + base
        hit = (col == owner) & (here < iota((LANES, size), 1))
        rank = rank + jnp.sum(jnp.where(hit, 1.0, 0.0), axis=0, keepdims=True)
    rank = rank.astype(jnp.int32)
    slot_ref[...] = owner * capacity + rank
    row = row_ref[...]
    high = (lax.shift_right_logical(row, 7) + 1).astype(jnp.float32)
    low = (row & 127).astype(jnp.float32)
    mine = iota((devices, size), 0) == owner
    place = one_hot((LANES, size), rank, 0)
    high = jnp.where(mine, high, 0.0).astype(jnp.bfloat16)
    low = jnp.where(mine, low, 0.0).astype(jnp.bfloat16)
    high = lax.dot_general(high, place, NT, preferred_element_type=jnp.float32)
    low = lax.dot_general(low, place, NT, preferred_element_type=jnp.float32)
    value = jnp.where(high > 0.5, (high - 1.0) * 128.0 + low, float(ROWS_DEV))
    ids_ref[...] = value.astype(jnp.int32)


def order_kernel(capacity, group, ids_ref, rank_ref, sorted_ref, count_ref):
    devices = ids_ref.shape[0]
    slots = devices * capacity
    chunks = slots // LANES
    ids = ids_ref[...]
    lane = iota((1, LANES), 1)
    rolled = {}
    rows = [jnp.zeros((1, LANES), jnp.int32) for _ in range(chunks)]
    for s in range(devices):
        at, off = divmod(s * capacity, LANES)
        if off not in rolled:
            rolled[off] = pltpu.roll(ids, off, 1) if off else ids
        piece = rolled[off][s : s + 1, :]
        rows[at] = jnp.where((lane >= off) & (lane < off + capacity), piece, rows[at])
        if off + capacity > LANES:
            rows[at + 1] = jnp.where(lane < off + capacity - LANES, piece, rows[at + 1])
    edges = lane * group
    count = jnp.zeros((1, LANES), jnp.float32)
    ranks = [jnp.zeros((1, LANES), jnp.float32) for _ in range(chunks)]
    earlier = iota((LANES, LANES), 0) < iota((LANES, LANES), 1)
    for j in range(chunks):
        col = column(rows[j])
        count = count + jnp.sum(jnp.where(col < edges, 1.0, 0.0), axis=0, keepdims=True)
        for i in range(chunks):
            if j < i:
                hit = col <= rows[i]
            elif j > i:
                hit = col < rows[i]
            else:
                hit = (col < rows[i]) | ((col == rows[i]) & earlier)
            ranks[i] = ranks[i] + jnp.sum(jnp.where(hit, 1.0, 0.0), axis=0, keepdims=True)
    count_ref[...] = count.astype(jnp.int32)
    rank = jnp.concatenate(ranks, axis=1).astype(jnp.int32)
    rank_ref[...] = rank
    row = jnp.concatenate(rows, axis=1)
    high = jnp.broadcast_to(lax.shift_right_logical(row, 7).astype(jnp.float32), (8, slots)).astype(jnp.bfloat16)
    low = jnp.broadcast_to((row & 127).astype(jnp.float32), (8, slots)).astype(jnp.bfloat16)
    for c in range(chunks):
        pick = one_hot((LANES, slots), rank, c * LANES)
        up = lax.dot_general(high, pick, NT, preferred_element_type=jnp.float32)
        down = lax.dot_general(low, pick, NT, preferred_element_type=jnp.float32)
        sorted_ref[c : c + 1, :] = (up * 128.0 + down)[0:1, :].astype(jnp.int32)


def stats_kernel(scale, blocks, olds, final, *refs):
    q_ref = refs[0]
    k_refs = refs[1 : 1 + blocks]
    old = refs[1 + blocks : 1 + blocks + olds]
    outs = refs[1 + blocks + olds :]
    size = q_ref.shape[0]
    for base in range(0, size, SUB):
        at = slice(base, base + SUB)
        q = q_ref[at, :]
        top = old[0][:, at] if old else None
        total = old[1][:, at] if old else None
        for k in k_refs:
            scores = scale * lax.dot_general(k[...], q, NT, preferred_element_type=jnp.float32)
            high = jnp.max(scores, axis=0, keepdims=True)
            high = high if top is None else jnp.maximum(top, high)
            part = jnp.sum(jnp.exp2(scores - high), axis=0, keepdims=True)
            total = part if top is None else total * jnp.exp2(top - high) + part
            top = high
        if final:
            outs[0][:, at] = top + jnp.log2(total)
        else:
            outs[0][:, at] = top
            outs[1][:, at] = total


def query_kernel(scale, blocks, q_ref, lse_ref, pos_ref, *refs):
    k_refs, out_ref = refs[:blocks], refs[-1]
    size = q_ref.shape[0]
    for base in range(0, size, SUB):
        at = slice(base, base + SUB)
        q = q_ref[at, :]
        total = None
        for m, k in enumerate(k_refs):
            scores = (scale * LOG2E) * lax.dot_general(k[...], q, NT, preferred_element_type=jnp.float32)
            weights = jnp.exp2(scores - lse_ref[:, at])
            if m == 0:
                weights = weights - jnp.where(iota((size, SUB), 0) == pos_ref[:, at], 1.0, 0.0)
            part = lax.dot_general(weights.astype(jnp.bfloat16), k[...], TN, preferred_element_type=jnp.float32)
            total = part if total is None else total + part
        out_ref[at, :] = (scale * total).astype(jnp.bfloat16)


def item_kernel(scale, own, last, k_ref, q_ref, lse_ref, *refs):
    refs = list(refs)
    size = k_ref.shape[0]
    keys = k_ref[...]
    pos = refs.pop(0)[...] if own else None
    total = None if own else refs.pop(0)[...]
    for base in range(0, size, SUB):
        at = slice(base, base + SUB)
        q = q_ref[at, :]
        scores = (scale * LOG2E) * lax.dot_general(keys, q, NT, preferred_element_type=jnp.float32)
        weights = jnp.exp2(scores - lse_ref[:, at])
        if own:
            weights = weights - jnp.where(iota((size, SUB), 0) == pos[:, at], 1.0, 0.0)
        part = jnp.dot(weights.astype(jnp.bfloat16), q, preferred_element_type=jnp.float32)
        total = part if total is None else total + part
    if not last:
        refs[0][...] = total
        return
    slot_ref, out_ref, send_ref = refs
    grad = (scale * total).astype(jnp.bfloat16)
    out_ref[...] = grad
    for base in range(0, send_ref.shape[0], SUB):
        pick = one_hot((SUB, size), slot_ref[...], base)
        part = jnp.dot(pick, grad, preferred_element_type=jnp.float32)
        send_ref[base : base + SUB, :] = part.astype(jnp.bfloat16)


def table_kernel(groups, count_ref, rows_ref, rank_ref, sorted_ref, out_ref, pick, arranged, table, total, done):
    chunks = arranged.shape[0] // LANES
    width = rows_ref.shape[1]
    steps = table.shape[0] // (groups * SUB)
    for at in range(0, chunks * LANES, SUB):
        pick[at : at + SUB, :] = one_hot((SUB, chunks * LANES), rank_ref[...], at)
    arranged[...] = jnp.dot(pick[...], rows_ref[...], preferred_element_type=jnp.float32).astype(jnp.bfloat16)

    def spread(chunk, base):
        at = pl.multiple_of(chunk * LANES, LANES)
        ids = jnp.concatenate([sorted_ref[pl.ds(chunk, 1), :], sorted_ref[pl.ds(chunk + 1, 1), :]], axis=1)
        hot = one_hot((SUB, 2 * LANES), ids - base, 0)
        return jnp.dot(hot, arranged[pl.ds(at, 2 * LANES), :], preferred_element_type=jnp.float32)

    def copy_out(step):
        at = pl.ds(pl.multiple_of(step * (groups * SUB), groups * SUB), groups * SUB)
        return pltpu.make_async_copy(table.at[at, :], out_ref.at[at, :], done.at[step])

    def one_step(step, carry):
        firsts = [jnp.minimum(count_ref[step * groups + g] // LANES, chunks - 2) for g in range(groups)]
        overs = [count_ref[step * groups + g + 1] > (firsts[g] + 2) * LANES for g in range(groups)]
        for g in range(groups):
            base = (step * groups + g) * SUB
            at = pl.ds(pl.multiple_of(base, SUB), SUB)
            table[at, :] = spread(firsts[g], base).astype(jnp.bfloat16)

        @pl.when(functools.reduce(jnp.logical_or, overs))
        def _():
            def group(g, inner):
                base = (step * groups + g) * SUB
                total[...] = jnp.zeros((SUB, width), jnp.float32)

                def more(pair, deeper):
                    total[...] += spread(2 * pair, base)
                    return deeper

                lax.fori_loop(0, chunks // 2, more, 0)
                table[pl.ds(pl.multiple_of(base, SUB), SUB), :] = total[...].astype(jnp.bfloat16)
                return inner

            lax.fori_loop(0, groups, group, 0)

        copy_out(step).start()
        return carry

    lax.fori_loop(0, steps, one_step, 0)

    def finish(step, carry):
        copy_out(step).wait()
        return carry

    lax.fori_loop(0, steps, finish, 0)


def local(queries, items, positives, item_owner, item_row):
    size, width = queries.shape
    scale = 3.0 / math.sqrt(width)
    blk_count = lax.axis_size("blk")
    window = blk_count // 2
    devices = blk_count * lax.axis_size("table")
    capacity = -(-(3 * size // devices) // 8) * 8
    slots = devices * capacity
    f32 = functools.partial(jax.ShapeDtypeStruct, dtype=jnp.float32)
    b16 = functools.partial(jax.ShapeDtypeStruct, dtype=jnp.bfloat16)
    i32 = functools.partial(jax.ShapeDtypeStruct, dtype=jnp.int32)

    owner_row = item_owner.reshape(1, size)
    row_row = item_row.reshape(1, size)
    pos_row = positives.reshape(1, size)

    pair = 2 * size * size * width
    twos = range(1, window // 2)
    k_two = [moved(items, "blk", lambda i, j=j: i + 2 * j) for j in twos]
    k_odd = moved(items, "blk", lambda i: i + window - 1 if i % 2 else i + 1)
    q_two = [moved(queries, "blk", lambda i, j=j: i - 2 * j) for j in twos]
    q_odd = moved(queries, "blk", lambda i: i - 1 if i % 2 else i - (window - 1))
    slot, ids, top, total, pos_row, queries, items = pl.pallas_call(
        functools.partial(first_kernel, scale * LOG2E, devices, capacity),
        out_shape=(
            i32((1, size)),
            i32((devices, LANES)),
            f32((1, size)),
            f32((1, size)),
            i32((1, size)),
            b16((size, width)),
            b16((size, width)),
        ),
        in_specs=[pl.BlockSpec(memory_space=pltpu.HBM) for _ in range(5)],
        out_specs=tuple(vmem() for _ in range(7)),
        scratch_shapes=[
            pltpu.VMEM((1, size), jnp.int32),
            pltpu.VMEM((1, size), jnp.int32),
            pltpu.SemaphoreType.DMA((5,)),
        ],
        compiler_params=params(12),
        cost_estimate=pl.CostEstimate(flops=pair, bytes_accessed=4 * size * width, transcendentals=size * size),
    )(*[pltpu.with_memory_space_constraint(x, pltpu.HBM) for x in (owner_row, row_row, items, queries, pos_row)])
    got_ids = lax.all_to_all(
        ids.reshape(devices, 1, LANES), ("blk", "table"), split_axis=0, concat_axis=0, tiled=True
    ).reshape(devices, LANES)
    k_swap = [moved(k, "blk", lambda i: i ^ 1) for k in k_two]
    q_swap = [moved(q, "blk", lambda i: i ^ 1) for q in q_two]
    k_all = [k_odd, *k_two, *k_swap]
    q_all = [*q_two, q_odd, *q_swap]
    table_groups = ROWS_DEV // SUB
    early = [k_odd, *k_two]
    top, total = call(
        functools.partial(stats_kernel, scale * LOG2E, len(early), 2, False),
        (f32((1, size)), f32((1, size))),
        (queries, *early, top, total),
        flops=pair * len(early),
        trans=size * size * len(early),
    )
    lse = call(
        functools.partial(stats_kernel, scale * LOG2E, len(k_swap), 2, True),
        f32((1, size)),
        (queries, *k_swap, top, total),
        flops=pair * len(k_swap),
        trans=size * size * len(k_swap),
    )
    got_rank, got_sorted, got_count = call(
        functools.partial(order_kernel, capacity, SUB),
        (i32((1, slots)), i32((slots // LANES, LANES)), i32((1, LANES))),
        (got_ids,),
        flops=32 * slots * slots,
    )
    lse_odd = moved(lse, "blk", lambda i: i - 1 if i % 2 else i - (window - 1))
    lse_two = [moved(lse, "blk", lambda i, j=j: i - 2 * j) for j in twos]
    lse_swap = [moved(lse, "blk", lambda i, j=j: (i ^ 1) - 2 * j) for j in twos]
    lse_all = [*lse_two, lse_odd, *lse_swap]

    query_grad = call(
        functools.partial(query_kernel, scale, window),
        b16((size, width)),
        (queries, lse, pos_row, items, *k_all),
        flops=2 * pair * window,
        trans=size * size * window,
    )
    item_sum = call(
        functools.partial(item_kernel, scale, True, False),
        f32((size, width)),
        (items, queries, lse, pos_row),
        flops=2 * pair,
        trans=size * size,
    )
    for q, one in zip(q_all[:-1], lse_all[:-1]):
        item_sum = call(
            functools.partial(item_kernel, scale, False, False),
            f32((size, width)),
            (items, q, one, item_sum),
            flops=2 * pair,
            trans=size * size,
        )
    item_grad, send_rows = call(
        functools.partial(item_kernel, scale, False, True),
        (b16((size, width)), b16((slots, width))),
        (items, q_all[-1], lse_all[-1], item_sum, slot),
        flops=2 * pair + 2 * slots * size * width,
        trans=size * size,
    )
    got_rows = lax.all_to_all(
        send_rows.reshape(devices, capacity, width), ("blk", "table"), split_axis=0, concat_axis=0, tiled=True
    ).reshape(slots, width)
    groups = 8
    table_grad = pl.pallas_call(
        functools.partial(table_kernel, groups),
        out_shape=b16((ROWS_DEV, width)),
        in_specs=[pl.BlockSpec(memory_space=pltpu.SMEM), vmem(), vmem(), vmem()],
        out_specs=pl.BlockSpec(memory_space=pltpu.HBM),
        scratch_shapes=[
            pltpu.VMEM((slots, slots), jnp.bfloat16),
            pltpu.VMEM((slots, width), jnp.bfloat16),
            pltpu.VMEM((ROWS_DEV, width), jnp.bfloat16),
            pltpu.VMEM((SUB, width), jnp.float32),
            pltpu.SemaphoreType.DMA((table_groups // groups,)),
        ],
        compiler_params=params(32),
        cost_estimate=pl.CostEstimate(
            flops=2 * slots * slots * width, bytes_accessed=2 * ROWS_DEV * width, transcendentals=0
        ),
    )(got_count.reshape(LANES), got_rows, got_rank, got_sorted)
    return (query_grad, item_grad, table_grad)


def solution(mesh):
    both = P(("blk", "table"), None)
    flat = P(("blk", "table"))
    return jax.shard_map(
        local, mesh=mesh, in_specs=(both, both, flat, both, flat), out_specs=(both, both, both), check_vma=False
    )
```

```python
import functools
import math

import jax
import jax.numpy as jnp
from jax import lax
from jax.experimental import pallas as pl
from jax.experimental.pallas import tpu as pltpu
from jax.sharding import PartitionSpec as P


ROWS_DEV = 16384
LANES = 128
SUB = 256
PACK = 16
LOG2E = math.log2(math.e)
NT = (((1,), (1,)), ((), ()))
TN = (((0,), (0,)), ((), ()))


def moved(block, axis, target_of):
    count = lax.axis_size(axis)
    return lax.ppermute(block, axis, [(i, target_of(i) % count) for i in range(count)])


def vmem():
    return pl.BlockSpec(memory_space=pltpu.VMEM)


def params(mib):
    return pltpu.CompilerParams(vmem_limit_bytes=mib * 2**20)


def call(body, out_shape, args, flops=0, trans=0, mib=12):
    moved_bytes = sum(a.size * a.dtype.itemsize for a in args)
    outs = out_shape if isinstance(out_shape, (tuple, list)) else (out_shape,)
    moved_bytes += sum(math.prod(o.shape) * o.dtype.itemsize for o in outs)
    specs = [vmem() for _ in outs]
    return pl.pallas_call(
        body,
        out_shape=out_shape,
        in_specs=[vmem() for _ in args],
        out_specs=specs if isinstance(out_shape, (tuple, list)) else specs[0],
        cost_estimate=pl.CostEstimate(flops=flops, bytes_accessed=moved_bytes, transcendentals=trans),
        compiler_params=params(mib),
    )(*args)


def iota(shape, dim, dtype=jnp.int32):
    value = lax.broadcasted_iota(jnp.int32, shape, dim)
    return value if dtype == jnp.int32 else value.astype(dtype)


def column(row):
    wide = jnp.broadcast_to(row, (LANES, LANES))
    return jnp.transpose(wide)


def one_hot(shape, row, base):
    there = (iota(shape, 0) + base).astype(jnp.int16)
    return jnp.where(there == row.astype(jnp.int16), jnp.bfloat16(1), jnp.bfloat16(0))


def first_kernel(scale, devices, capacity, *refs):
    sources, results, (owner_ref, row_ref, done) = refs[:5], refs[5:12], refs[12:]
    slot_ref, ids_ref, top_ref, total_ref, pos_ref, q_ref, k_ref = results
    targets = (owner_ref, row_ref, k_ref, q_ref, pos_ref)
    copies = [pltpu.make_async_copy(a, b, done.at[i]) for i, (a, b) in enumerate(zip(sources, targets))]
    for copy in copies:
        copy.start()
    copies[0].wait()
    copies[1].wait()
    route(devices, capacity, owner_ref, row_ref, slot_ref, ids_ref)
    copies[2].wait()
    copies[3].wait()
    stats_kernel(scale, 1, 0, False, q_ref, k_ref, top_ref, total_ref)
    copies[4].wait()


def route(devices, capacity, owner_ref, row_ref, slot_ref, ids_ref):
    size = owner_ref.shape[1]
    owner = owner_ref[...]
    rank = jnp.zeros((1, size), jnp.float32)
    for base in range(0, size, LANES):
        col = column(owner[:, base : base + LANES])
        col = jnp.concatenate([col] * (size // LANES), axis=1)
        here = iota((LANES, size), 0) + base
        hit = (col == owner) & (here < iota((LANES, size), 1))
        rank = rank + jnp.sum(jnp.where(hit, 1.0, 0.0), axis=0, keepdims=True)
    rank = rank.astype(jnp.int32)
    slot_ref[...] = owner * capacity + rank
    row = row_ref[...]
    high = (lax.shift_right_logical(row, 7) + 1).astype(jnp.float32)
    low = (row & 127).astype(jnp.float32)
    mine = iota((devices, size), 0) == owner
    place = one_hot((LANES, size), rank, 0)
    high = jnp.where(mine, high, 0.0).astype(jnp.bfloat16)
    low = jnp.where(mine, low, 0.0).astype(jnp.bfloat16)
    high = lax.dot_general(high, place, NT, preferred_element_type=jnp.float32)
    low = lax.dot_general(low, place, NT, preferred_element_type=jnp.float32)
    value = jnp.where(high > 0.5, (high - 1.0) * 128.0 + low, float(ROWS_DEV))
    ids_ref[...] = value.astype(jnp.int32)


def order_kernel(capacity, group, groups, ids_ref, rank_ref, sorted_ref, count_ref):
    devices = ids_ref.shape[0]
    slots = devices * capacity
    chunks = slots // LANES
    ids = ids_ref[...]
    lane = iota((1, LANES), 1)
    rolled = {}
    rows = [jnp.zeros((1, LANES), jnp.int32) for _ in range(chunks)]
    for s in range(devices):
        at, off = divmod(s * capacity, LANES)
        if off not in rolled:
            rolled[off] = pltpu.roll(ids, off, 1) if off else ids
        piece = rolled[off][s : s + 1, :]
        rows[at] = jnp.where((lane >= off) & (lane < off + capacity), piece, rows[at])
        if off + capacity > LANES:
            rows[at + 1] = jnp.where(lane < off + capacity - LANES, piece, rows[at + 1])
    edges = lane * group
    count = jnp.zeros((1, LANES), jnp.float32)
    ranks = [jnp.zeros((1, LANES), jnp.float32) for _ in range(chunks)]
    earlier = iota((LANES, LANES), 0) < iota((LANES, LANES), 1)
    for j in range(chunks):
        col = column(rows[j])
        count = count + jnp.sum(jnp.where(col < edges, 1.0, 0.0), axis=0, keepdims=True)
        for i in range(chunks):
            if j < i:
                hit = col <= rows[i]
            elif j > i:
                hit = col < rows[i]
            else:
                hit = (col < rows[i]) | ((col == rows[i]) & earlier)
            ranks[i] = ranks[i] + jnp.sum(jnp.where(hit, 1.0, 0.0), axis=0, keepdims=True)
    count = count.astype(jnp.int32)
    covered = start_of(count, slots) + LANES
    over = (pltpu.roll(count, LANES - 1, 1) > covered) & (lane < groups)
    over = jnp.max(jnp.where(over, 1.0, 0.0), axis=1, keepdims=True).astype(jnp.int32)
    count_ref[...] = jnp.where(lane == LANES - 1, over, count)
    rank = jnp.concatenate(ranks, axis=1).astype(jnp.int32)
    rank_ref[...] = rank
    row = jnp.concatenate(rows, axis=1)
    high = jnp.broadcast_to(lax.shift_right_logical(row, 7).astype(jnp.float32), (8, slots)).astype(jnp.bfloat16)
    low = jnp.broadcast_to((row & 127).astype(jnp.float32), (8, slots)).astype(jnp.bfloat16)
    lines = []
    for c in range(chunks):
        pick = one_hot((LANES, slots), rank, c * LANES)
        up = lax.dot_general(high, pick, NT, preferred_element_type=jnp.float32)
        down = lax.dot_general(low, pick, NT, preferred_element_type=jnp.float32)
        lines.append((up * 128.0 + down)[0:1, :].astype(jnp.int32))
    for o in range(LANES // PACK):
        turned = [pltpu.roll(line, LANES - o * PACK, 1) if o else line for line in lines]
        for c in range(chunks):
            after_it = turned[min(c + 1, chunks - 1)]
            sorted_ref[o, c : c + 1, :] = jnp.where(lane < LANES - o * PACK, turned[c], after_it)


def start_of(count, slots):
    packs = lax.shift_right_logical(count, PACK.bit_length() - 1)
    return jnp.minimum(packs * PACK, slots - LANES)


def stats_kernel(scale, blocks, olds, final, *refs):
    q_ref = refs[0]
    k_refs = refs[1 : 1 + blocks]
    old = refs[1 + blocks : 1 + blocks + olds]
    outs = refs[1 + blocks + olds :]
    size = q_ref.shape[0]
    for base in range(0, size, SUB):
        at = slice(base, base + SUB)
        q = q_ref[at, :]
        top = old[0][:, at] if old else None
        total = old[1][:, at] if old else None
        for k in k_refs:
            scores = scale * lax.dot_general(k[...], q, NT, preferred_element_type=jnp.float32)
            high = jnp.max(scores, axis=0, keepdims=True)
            high = high if top is None else jnp.maximum(top, high)
            part = jnp.sum(jnp.exp2(scores - high), axis=0, keepdims=True)
            total = part if top is None else total * jnp.exp2(top - high) + part
            top = high
        if final:
            outs[0][:, at] = top + jnp.log2(total)
        else:
            outs[0][:, at] = top
            outs[1][:, at] = total


def query_kernel(scale, blocks, q_ref, lse_ref, pos_ref, *refs):
    k_refs, out_ref = refs[:blocks], refs[-1]
    size = q_ref.shape[0]
    for base in range(0, size, SUB):
        at = slice(base, base + SUB)
        q = q_ref[at, :]
        total = None
        for m, k in enumerate(k_refs):
            scores = (scale * LOG2E) * lax.dot_general(k[...], q, NT, preferred_element_type=jnp.float32)
            weights = jnp.exp2(scores - lse_ref[:, at])
            if m == 0:
                weights = weights - jnp.where(iota((size, SUB), 0) == pos_ref[:, at], 1.0, 0.0)
            part = lax.dot_general(weights.astype(jnp.bfloat16), k[...], TN, preferred_element_type=jnp.float32)
            total = part if total is None else total + part
        out_ref[at, :] = (scale * total).astype(jnp.bfloat16)


def item_kernel(scale, own, last, k_ref, q_ref, lse_ref, *refs):
    refs = list(refs)
    size = k_ref.shape[0]
    keys = k_ref[...]
    pos = refs.pop(0)[...] if own else None
    total = None if own else refs.pop(0)[...]
    for base in range(0, size, SUB):
        at = slice(base, base + SUB)
        q = q_ref[at, :]
        scores = (scale * LOG2E) * lax.dot_general(keys, q, NT, preferred_element_type=jnp.float32)
        weights = jnp.exp2(scores - lse_ref[:, at])
        if own:
            weights = weights - jnp.where(iota((size, SUB), 0) == pos[:, at], 1.0, 0.0)
        part = jnp.dot(weights.astype(jnp.bfloat16), q, preferred_element_type=jnp.float32)
        total = part if total is None else total + part
    if not last:
        refs[0][...] = total
        return
    slot_ref, out_ref, send_ref = refs
    grad = (scale * total).astype(jnp.bfloat16)
    out_ref[...] = grad
    pick = one_hot((send_ref.shape[0], size), slot_ref[...], 0)
    send_ref[...] = jnp.dot(pick, grad, preferred_element_type=jnp.float32).astype(jnp.bfloat16)


def table_kernel(group, per_copy, count_ref, rows_ref, rank_ref, sorted_ref, out_ref, pick, arranged, table, total, done):
    slots, width = arranged.shape
    groups = table.shape[0] // group
    copies = groups // per_copy
    for at in range(0, slots, SUB):
        pick[at : at + SUB, :] = one_hot((SUB, slots), rank_ref[...], at)
    arranged[...] = jnp.dot(pick[...], rows_ref[...], preferred_element_type=jnp.float32).astype(jnp.bfloat16)

    def spread(start, base):
        turn = lax.shift_right_logical(start, PACK.bit_length() - 1) & (LANES // PACK - 1)
        ids = sorted_ref[turn, pl.ds(lax.shift_right_logical(start, 7), 1), :]
        hot = one_hot((group, LANES), ids - base, 0)
        at = pl.ds(pl.multiple_of(start, PACK), LANES)
        return jnp.dot(hot, arranged[at, :], preferred_element_type=jnp.float32)

    def copy_out(c):
        size = per_copy * group
        at = pl.ds(c * size if isinstance(c, int) else pl.multiple_of(c * size, size), size)
        return pltpu.make_async_copy(table.at[at, :], out_ref.at[at, :], done.at[c])

    over = count_ref[LANES - 1] > 0

    @pl.when(jnp.logical_not(over))
    def _():
        for c in range(copies):
            for number in range(c * per_copy, (c + 1) * per_copy):
                start = start_of(count_ref[number], slots)
                table[number * group : (number + 1) * group, :] = spread(start, number * group).astype(jnp.bfloat16)
            copy_out(c).start()

    @pl.when(over)
    def _():
        def one(c, carry):
            def each(g, inner):
                number = c * per_copy + g
                total[...] = jnp.zeros((group, width), jnp.float32)

                def more(chunk, deeper):
                    total[...] += spread(chunk * LANES, number * group)
                    return deeper

                lax.fori_loop(0, slots // LANES, more, 0)
                table[pl.ds(pl.multiple_of(number * group, group), group), :] = total[...].astype(jnp.bfloat16)
                return inner

            lax.fori_loop(0, per_copy, each, 0)
            copy_out(c).start()
            return carry

        lax.fori_loop(0, copies, one, 0)

    for c in range(copies):
        copy_out(c).wait()


def local(queries, items, positives, item_owner, item_row):
    size, width = queries.shape
    scale = 3.0 / math.sqrt(width)
    blk_count = lax.axis_size("blk")
    window = blk_count // 2
    devices = blk_count * lax.axis_size("table")
    capacity = -(-(3 * size // devices) // 8) * 8
    slots = devices * capacity
    f32 = functools.partial(jax.ShapeDtypeStruct, dtype=jnp.float32)
    b16 = functools.partial(jax.ShapeDtypeStruct, dtype=jnp.bfloat16)
    i32 = functools.partial(jax.ShapeDtypeStruct, dtype=jnp.int32)

    owner_row = item_owner.reshape(1, size)
    row_row = item_row.reshape(1, size)
    pos_row = positives.reshape(1, size)

    pair = 2 * size * size * width
    twos = range(1, window // 2)
    k_two = [moved(items, "blk", lambda i, j=j: i + 2 * j) for j in twos]
    k_odd = moved(items, "blk", lambda i: i + window - 1 if i % 2 else i + 1)
    q_two = [moved(queries, "blk", lambda i, j=j: i - 2 * j) for j in twos]
    q_odd = moved(queries, "blk", lambda i: i - 1 if i % 2 else i - (window - 1))
    slot, ids, top, total, pos_row, queries, items = pl.pallas_call(
        functools.partial(first_kernel, scale * LOG2E, devices, capacity),
        out_shape=(
            i32((1, size)),
            i32((devices, LANES)),
            f32((1, size)),
            f32((1, size)),
            i32((1, size)),
            b16((size, width)),
            b16((size, width)),
        ),
        in_specs=[pl.BlockSpec(memory_space=pltpu.HBM) for _ in range(5)],
        out_specs=tuple(vmem() for _ in range(7)),
        scratch_shapes=[
            pltpu.VMEM((1, size), jnp.int32),
            pltpu.VMEM((1, size), jnp.int32),
            pltpu.SemaphoreType.DMA((5,)),
        ],
        compiler_params=params(12),
        cost_estimate=pl.CostEstimate(flops=pair, bytes_accessed=4 * size * width, transcendentals=size * size),
    )(*[pltpu.with_memory_space_constraint(x, pltpu.HBM) for x in (owner_row, row_row, items, queries, pos_row)])
    got_ids = lax.all_to_all(
        ids.reshape(devices, 1, LANES), ("blk", "table"), split_axis=0, concat_axis=0, tiled=True
    ).reshape(devices, LANES)
    k_swap = [moved(k, "blk", lambda i: i ^ 1) for k in k_two]
    q_swap = [moved(q, "blk", lambda i: i ^ 1) for q in q_two]
    k_all = [k_odd, *k_two, *k_swap]
    q_all = [*q_two, q_odd, *q_swap]
    early = [k_odd, *k_two]
    top, total = call(
        functools.partial(stats_kernel, scale * LOG2E, len(early), 2, False),
        (f32((1, size)), f32((1, size))),
        (queries, *early, top, total),
        flops=pair * len(early),
        trans=size * size * len(early),
    )
    lse = call(
        functools.partial(stats_kernel, scale * LOG2E, len(k_swap), 2, True),
        f32((1, size)),
        (queries, *k_swap, top, total),
        flops=pair * len(k_swap),
        trans=size * size * len(k_swap),
    )
    group, per_copy = 512, 4
    got_rank, got_sorted, got_count = call(
        functools.partial(order_kernel, capacity, group, ROWS_DEV // group),
        (i32((1, slots)), i32((LANES // PACK, slots // LANES, LANES)), i32((1, LANES))),
        (got_ids,),
        flops=32 * slots * slots,
    )
    lse_odd = moved(lse, "blk", lambda i: i - 1 if i % 2 else i - (window - 1))
    lse_two = [moved(lse, "blk", lambda i, j=j: i - 2 * j) for j in twos]
    lse_swap = [moved(lse, "blk", lambda i, j=j: (i ^ 1) - 2 * j) for j in twos]
    lse_all = [*lse_two, lse_odd, *lse_swap]

    query_grad = call(
        functools.partial(query_kernel, scale, window),
        b16((size, width)),
        (queries, lse, pos_row, items, *k_all),
        flops=2 * pair * window,
        trans=size * size * window,
    )
    item_sum = call(
        functools.partial(item_kernel, scale, True, False),
        f32((size, width)),
        (items, queries, lse, pos_row),
        flops=2 * pair,
        trans=size * size,
    )
    for q, one in zip(q_all[:-1], lse_all[:-1]):
        item_sum = call(
            functools.partial(item_kernel, scale, False, False),
            f32((size, width)),
            (items, q, one, item_sum),
            flops=2 * pair,
            trans=size * size,
        )
    item_grad, send_rows = call(
        functools.partial(item_kernel, scale, False, True),
        (b16((size, width)), b16((slots, width))),
        (items, q_all[-1], lse_all[-1], item_sum, slot),
        flops=2 * pair + 2 * slots * size * width,
        trans=size * size,
    )
    got_rows = lax.all_to_all(
        send_rows.reshape(devices, capacity, width), ("blk", "table"), split_axis=0, concat_axis=0, tiled=True
    ).reshape(slots, width)
    table_grad = pl.pallas_call(
        functools.partial(table_kernel, group, per_copy),
        out_shape=b16((ROWS_DEV, width)),
        in_specs=[pl.BlockSpec(memory_space=pltpu.SMEM), vmem(), vmem(), vmem()],
        out_specs=pl.BlockSpec(memory_space=pltpu.HBM),
        scratch_shapes=[
            pltpu.VMEM((slots, slots), jnp.bfloat16),
            pltpu.VMEM((slots, width), jnp.bfloat16),
            pltpu.VMEM((ROWS_DEV, width), jnp.bfloat16),
            pltpu.VMEM((group, width), jnp.float32),
            pltpu.SemaphoreType.DMA((ROWS_DEV // (group * per_copy),)),
        ],
        compiler_params=params(32),
        cost_estimate=pl.CostEstimate(
            flops=2 * slots * slots * width, bytes_accessed=2 * ROWS_DEV * width, transcendentals=0
        ),
    )(got_count.reshape(LANES), got_rows, got_rank, got_sorted)
    return (query_grad, item_grad, table_grad)


def solution(mesh):
    both = P(("blk", "table"), None)
    flat = P(("blk", "table"))
    return jax.shard_map(
        local, mesh=mesh, in_specs=(both, both, flat, both, flat), out_specs=(both, both, both), check_vma=False
    )
```

```python
import functools
import math

import jax
import jax.numpy as jnp
from jax import lax
from jax.experimental import pallas as pl
from jax.experimental.pallas import tpu as pltpu
from jax.sharding import PartitionSpec as P


ROWS_DEV = 16384
LANES = 128
SUB = 256
PACK = 16
LOG2E = math.log2(math.e)
NT = (((1,), (1,)), ((), ()))
TN = (((0,), (0,)), ((), ()))


def moved(block, axis, target_of):
    count = lax.axis_size(axis)
    return lax.ppermute(block, axis, [(i, target_of(i) % count) for i in range(count)])


def vmem():
    return pl.BlockSpec(memory_space=pltpu.VMEM)


def params(mib):
    return pltpu.CompilerParams(vmem_limit_bytes=mib * 2**20)


def call(body, out_shape, args, flops=0, trans=0, mib=12):
    moved_bytes = sum(a.size * a.dtype.itemsize for a in args)
    outs = out_shape if isinstance(out_shape, (tuple, list)) else (out_shape,)
    moved_bytes += sum(math.prod(o.shape) * o.dtype.itemsize for o in outs)
    specs = [vmem() for _ in outs]
    return pl.pallas_call(
        body,
        out_shape=out_shape,
        in_specs=[pl.BlockSpec(memory_space=pltpu.SMEM) if a.size == 1 else vmem() for a in args],
        out_specs=specs if isinstance(out_shape, (tuple, list)) else specs[0],
        cost_estimate=pl.CostEstimate(flops=flops, bytes_accessed=moved_bytes, transcendentals=trans),
        compiler_params=params(mib),
    )(*args)


def iota(shape, dim, dtype=jnp.int32):
    value = lax.broadcasted_iota(jnp.int32, shape, dim)
    return value if dtype == jnp.int32 else value.astype(dtype)


def column(row):
    wide = jnp.broadcast_to(row, (LANES, LANES))
    return jnp.transpose(wide)


def one_hot(shape, row, base):
    there = (iota(shape, 0) + base).astype(jnp.int16)
    return jnp.where(there == row.astype(jnp.int16), jnp.bfloat16(1), jnp.bfloat16(0))


def first_kernel(devices, capacity, *refs):
    sources, results, (owner_ref, row_ref, done) = refs[:5], refs[5:10], refs[10:]
    slot_ref, ids_ref, pos_ref, q_ref, k_ref = results
    targets = (owner_ref, row_ref, k_ref, q_ref, pos_ref)
    copies = [pltpu.make_async_copy(a, b, done.at[i]) for i, (a, b) in enumerate(zip(sources, targets))]
    for copy in copies:
        copy.start()
    copies[0].wait()
    copies[1].wait()
    route(devices, capacity, owner_ref, row_ref, slot_ref, ids_ref)
    for copy in copies[2:]:
        copy.wait()


def route(devices, capacity, owner_ref, row_ref, slot_ref, ids_ref):
    size = owner_ref.shape[1]
    owner = owner_ref[...]
    rank = jnp.zeros((1, size), jnp.float32)
    for base in range(0, size, LANES):
        col = column(owner[:, base : base + LANES])
        col = jnp.concatenate([col] * (size // LANES), axis=1)
        here = iota((LANES, size), 0) + base
        hit = (col == owner) & (here < iota((LANES, size), 1))
        rank = rank + jnp.sum(jnp.where(hit, 1.0, 0.0), axis=0, keepdims=True)
    rank = rank.astype(jnp.int32)
    slot_ref[...] = owner * capacity + rank
    row = row_ref[...]
    high = (lax.shift_right_logical(row, 7) + 1).astype(jnp.float32)
    low = (row & 127).astype(jnp.float32)
    mine = iota((devices, size), 0) == owner
    place = one_hot((LANES, size), rank, 0)
    high = jnp.where(mine, high, 0.0).astype(jnp.bfloat16)
    low = jnp.where(mine, low, 0.0).astype(jnp.bfloat16)
    high = lax.dot_general(high, place, NT, preferred_element_type=jnp.float32)
    low = lax.dot_general(low, place, NT, preferred_element_type=jnp.float32)
    value = jnp.where(high > 0.5, (high - 1.0) * 128.0 + low, float(ROWS_DEV))
    ids_ref[...] = value.astype(jnp.int32)


def order_kernel(capacity, group, groups, tables, place_ref, *refs):
    parts, (rank_ref, sorted_ref, count_ref) = refs[:tables], refs[tables:]
    devices = tables * parts[0].shape[0]
    slots = devices * capacity
    chunks = slots // LANES
    lane = iota((1, LANES), 1)
    place = place_ref[0, 0]
    sources = []
    for t in range(tables):
        found = parts[0][...]
        for d in range(1, tables):
            found = jnp.where(lax.rem(place - d + tables, tables) == t, parts[d][...], found)
        sources.append(found)
    rolled = {}
    rows = [jnp.zeros((1, LANES), jnp.int32) for _ in range(chunks)]
    for s in range(devices):
        at, off = divmod(s * capacity, LANES)
        block, table = divmod(s, tables)
        if (off, table) not in rolled:
            rolled[off, table] = pltpu.roll(sources[table], off, 1) if off else sources[table]
        piece = rolled[off, table][block : block + 1, :]
        rows[at] = jnp.where((lane >= off) & (lane < off + capacity), piece, rows[at])
        if off + capacity > LANES:
            rows[at + 1] = jnp.where(lane < off + capacity - LANES, piece, rows[at + 1])
    edges = lane * group
    count = jnp.zeros((1, LANES), jnp.float32)
    ranks = [jnp.zeros((1, LANES), jnp.float32) for _ in range(chunks)]
    earlier = iota((LANES, LANES), 0) < iota((LANES, LANES), 1)
    for j in range(chunks):
        col = column(rows[j])
        count = count + jnp.sum(jnp.where(col < edges, 1.0, 0.0), axis=0, keepdims=True)
        for i in range(chunks):
            if j < i:
                hit = col <= rows[i]
            elif j > i:
                hit = col < rows[i]
            else:
                hit = (col < rows[i]) | ((col == rows[i]) & earlier)
            ranks[i] = ranks[i] + jnp.sum(jnp.where(hit, 1.0, 0.0), axis=0, keepdims=True)
    count = count.astype(jnp.int32)
    covered = start_of(count, slots) + LANES
    over = (pltpu.roll(count, LANES - 1, 1) > covered) & (lane < groups)
    over = jnp.max(jnp.where(over, 1.0, 0.0), axis=1, keepdims=True).astype(jnp.int32)
    count_ref[...] = jnp.where(lane == LANES - 1, over, count)
    rank = jnp.concatenate(ranks, axis=1).astype(jnp.int32)
    rank_ref[...] = rank
    row = jnp.concatenate(rows, axis=1)
    high = jnp.broadcast_to(lax.shift_right_logical(row, 7).astype(jnp.float32), (8, slots)).astype(jnp.bfloat16)
    low = jnp.broadcast_to((row & 127).astype(jnp.float32), (8, slots)).astype(jnp.bfloat16)
    lines = []
    for c in range(chunks):
        pick = one_hot((LANES, slots), rank, c * LANES)
        up = lax.dot_general(high, pick, NT, preferred_element_type=jnp.float32)
        down = lax.dot_general(low, pick, NT, preferred_element_type=jnp.float32)
        lines.append((up * 128.0 + down)[0:1, :].astype(jnp.int32))
    for o in range(LANES // PACK):
        turned = [pltpu.roll(line, LANES - o * PACK, 1) if o else line for line in lines]
        for c in range(chunks):
            after_it = turned[min(c + 1, chunks - 1)]
            sorted_ref[o, c : c + 1, :] = jnp.where(lane < LANES - o * PACK, turned[c], after_it)


def start_of(count, slots):
    packs = lax.shift_right_logical(count, PACK.bit_length() - 1)
    return jnp.minimum(packs * PACK, slots - LANES)


def stats_kernel(scale, blocks, olds, final, *refs):
    q_ref = refs[0]
    k_refs = refs[1 : 1 + blocks]
    old = refs[1 + blocks : 1 + blocks + olds]
    outs = refs[1 + blocks + olds :]
    size = q_ref.shape[0]
    for base in range(0, size, SUB):
        at = slice(base, base + SUB)
        q = q_ref[at, :]
        top = old[0][:, at] if old else None
        total = old[1][:, at] if old else None
        for k in k_refs:
            scores = scale * lax.dot_general(k[...], q, NT, preferred_element_type=jnp.float32)
            high = jnp.max(scores, axis=0, keepdims=True)
            high = high if top is None else jnp.maximum(top, high)
            part = jnp.sum(jnp.exp2(scores - high), axis=0, keepdims=True)
            total = part if top is None else total * jnp.exp2(top - high) + part
            top = high
        if final:
            outs[0][:, at] = top + jnp.log2(total)
        else:
            outs[0][:, at] = top
            outs[1][:, at] = total


def query_kernel(scale, blocks, q_ref, lse_ref, pos_ref, *refs):
    k_refs, out_ref = refs[:blocks], refs[-1]
    size = q_ref.shape[0]
    for base in range(0, size, SUB):
        at = slice(base, base + SUB)
        q = q_ref[at, :]
        total = None
        for m, k in enumerate(k_refs):
            scores = (scale * LOG2E) * lax.dot_general(k[...], q, NT, preferred_element_type=jnp.float32)
            weights = jnp.exp2(scores - lse_ref[:, at])
            if m == 0:
                weights = weights - jnp.where(iota((size, SUB), 0) == pos_ref[:, at], 1.0, 0.0)
            part = lax.dot_general(weights.astype(jnp.bfloat16), k[...], TN, preferred_element_type=jnp.float32)
            total = part if total is None else total + part
        out_ref[at, :] = (scale * total).astype(jnp.bfloat16)


def item_kernel(scale, own, last, k_ref, q_ref, lse_ref, *refs):
    refs = list(refs)
    size = k_ref.shape[0]
    keys = k_ref[...]
    pos = refs.pop(0)[...] if own else None
    total = None if own else refs.pop(0)[...]
    for base in range(0, size, SUB):
        at = slice(base, base + SUB)
        q = q_ref[at, :]
        scores = (scale * LOG2E) * lax.dot_general(keys, q, NT, preferred_element_type=jnp.float32)
        weights = jnp.exp2(scores - lse_ref[:, at])
        if own:
            weights = weights - jnp.where(iota((size, SUB), 0) == pos[:, at], 1.0, 0.0)
        part = jnp.dot(weights.astype(jnp.bfloat16), q, preferred_element_type=jnp.float32)
        total = part if total is None else total + part
    if not last:
        refs[0][...] = total
        return
    slot_ref, out_ref, send_ref = refs
    grad = (scale * total).astype(jnp.bfloat16)
    out_ref[...] = grad
    pick = one_hot((send_ref.shape[0], size), slot_ref[...], 0)
    send_ref[...] = jnp.dot(pick, grad, preferred_element_type=jnp.float32).astype(jnp.bfloat16)


def table_kernel(group, per_copy, count_ref, rows_ref, rank_ref, sorted_ref, out_ref, pick, arranged, table, total, done):
    slots, width = arranged.shape
    groups = table.shape[0] // group
    copies = groups // per_copy
    for at in range(0, slots, SUB):
        pick[at : at + SUB, :] = one_hot((SUB, slots), rank_ref[...], at)
    arranged[...] = jnp.dot(pick[...], rows_ref[...], preferred_element_type=jnp.float32).astype(jnp.bfloat16)

    def spread(start, base):
        turn = lax.shift_right_logical(start, PACK.bit_length() - 1) & (LANES // PACK - 1)
        ids = sorted_ref[turn, pl.ds(lax.shift_right_logical(start, 7), 1), :]
        hot = one_hot((group, LANES), ids - base, 0)
        at = pl.ds(pl.multiple_of(start, PACK), LANES)
        return jnp.dot(hot, arranged[at, :], preferred_element_type=jnp.float32)

    def copy_out(c):
        size = per_copy * group
        at = pl.ds(c * size if isinstance(c, int) else pl.multiple_of(c * size, size), size)
        return pltpu.make_async_copy(table.at[at, :], out_ref.at[at, :], done.at[c])

    over = count_ref[LANES - 1] > 0

    @pl.when(jnp.logical_not(over))
    def _():
        for c in range(copies):
            for number in range(c * per_copy, (c + 1) * per_copy):
                start = start_of(count_ref[number], slots)
                table[number * group : (number + 1) * group, :] = spread(start, number * group).astype(jnp.bfloat16)
            copy_out(c).start()

    @pl.when(over)
    def _():
        def one(c, carry):
            def each(g, inner):
                number = c * per_copy + g
                total[...] = jnp.zeros((group, width), jnp.float32)

                def more(chunk, deeper):
                    total[...] += spread(chunk * LANES, number * group)
                    return deeper

                lax.fori_loop(0, slots // LANES, more, 0)
                table[pl.ds(pl.multiple_of(number * group, group), group), :] = total[...].astype(jnp.bfloat16)
                return inner

            lax.fori_loop(0, per_copy, each, 0)
            copy_out(c).start()
            return carry

        lax.fori_loop(0, copies, one, 0)

    for c in range(copies):
        copy_out(c).wait()


def local(queries, items, positives, item_owner, item_row):
    size, width = queries.shape
    scale = 3.0 / math.sqrt(width)
    blk_count = lax.axis_size("blk")
    window = blk_count // 2
    table_count = lax.axis_size("table")
    devices = blk_count * table_count
    capacity = -(-(3 * size // devices) // 8) * 8
    slots = devices * capacity
    f32 = functools.partial(jax.ShapeDtypeStruct, dtype=jnp.float32)
    b16 = functools.partial(jax.ShapeDtypeStruct, dtype=jnp.bfloat16)
    i32 = functools.partial(jax.ShapeDtypeStruct, dtype=jnp.int32)

    owner_row = item_owner.reshape(1, size)
    row_row = item_row.reshape(1, size)
    pos_row = positives.reshape(1, size)

    pair = 2 * size * size * width
    twos = range(1, window // 2)
    k_two = [moved(items, "blk", lambda i, j=j: i + 2 * j) for j in twos]
    k_odd = moved(items, "blk", lambda i: i + window - 1 if i % 2 else i + 1)
    q_two = [moved(queries, "blk", lambda i, j=j: i - 2 * j) for j in twos]
    q_odd = moved(queries, "blk", lambda i: i - 1 if i % 2 else i - (window - 1))
    slot, ids, pos_row, queries, items = pl.pallas_call(
        functools.partial(first_kernel, devices, capacity),
        out_shape=(
            i32((1, size)),
            i32((devices, LANES)),
            i32((1, size)),
            b16((size, width)),
            b16((size, width)),
        ),
        in_specs=[pl.BlockSpec(memory_space=pltpu.HBM) for _ in range(5)],
        out_specs=tuple(vmem() for _ in range(5)),
        scratch_shapes=[
            pltpu.VMEM((1, size), jnp.int32),
            pltpu.VMEM((1, size), jnp.int32),
            pltpu.SemaphoreType.DMA((5,)),
        ],
        compiler_params=params(12),
        cost_estimate=pl.CostEstimate(flops=size * size, bytes_accessed=4 * size * width, transcendentals=0),
    )(*[pltpu.with_memory_space_constraint(x, pltpu.HBM) for x in (owner_row, row_row, items, queries, pos_row)])
    mine = lax.all_to_all(ids.reshape(blk_count, table_count, LANES), "blk", split_axis=0, concat_axis=0, tiled=True)
    k_swap = [moved(k, "blk", lambda i: i ^ 1) for k in k_two]
    q_swap = [moved(q, "blk", lambda i: i ^ 1) for q in q_two]
    k_all = [k_odd, *k_two, *k_swap]
    q_all = [*q_two, q_odd, *q_swap]
    early = [items, k_odd, *k_two]
    top, total = call(
        functools.partial(stats_kernel, scale * LOG2E, len(early), 0, False),
        (f32((1, size)), f32((1, size))),
        (queries, *early),
        flops=pair * len(early),
        trans=size * size * len(early),
    )
    lse = call(
        functools.partial(stats_kernel, scale * LOG2E, len(k_swap), 2, True),
        f32((1, size)),
        (queries, *k_swap, top, total),
        flops=pair * len(k_swap),
        trans=size * size * len(k_swap),
    )
    lse_odd = moved(lse, "blk", lambda i: i - 1 if i % 2 else i - (window - 1))
    lse_two = [moved(lse, "blk", lambda i, j=j: i - 2 * j) for j in twos]
    lse_swap = [moved(lse, "blk", lambda i, j=j: (i ^ 1) - 2 * j) for j in twos]
    lse_all = [*lse_two, lse_odd, *lse_swap]

    query_grad = call(
        functools.partial(query_kernel, scale, window),
        b16((size, width)),
        (queries, lse, pos_row, items, *k_all),
        flops=2 * pair * window,
        trans=size * size * window,
    )
    item_sum = call(
        functools.partial(item_kernel, scale, True, False),
        f32((size, width)),
        (items, queries, lse, pos_row),
        flops=2 * pair,
        trans=size * size,
    )
    for q, one in zip(q_all[:-1], lse_all[:-1]):
        item_sum = call(
            functools.partial(item_kernel, scale, False, False),
            f32((size, width)),
            (items, q, one, item_sum),
            flops=2 * pair,
            trans=size * size,
        )
    item_grad, send_rows = call(
        functools.partial(item_kernel, scale, False, True),
        (b16((size, width)), b16((slots, width))),
        (items, q_all[-1], lse_all[-1], item_sum, slot),
        flops=2 * pair + 2 * slots * size * width,
        trans=size * size,
    )
    got_rows = lax.all_to_all(
        send_rows.reshape(devices, capacity, width), ("blk", "table"), split_axis=0, concat_axis=0, tiled=True
    ).reshape(slots, width)
    place = lax.axis_index("table")
    parts = [lax.dynamic_index_in_dim(mine, place, 1, keepdims=False)]
    for d in range(1, table_count):
        part = lax.dynamic_index_in_dim(mine, (place + d) % table_count, 1, keepdims=False)
        parts.append(moved(part, "table", lambda i, d=d: i + d))
    group, per_copy = 512, 4
    got_rank, got_sorted, got_count = call(
        functools.partial(order_kernel, capacity, group, ROWS_DEV // group, table_count),
        (i32((1, slots)), i32((LANES // PACK, slots // LANES, LANES)), i32((1, LANES))),
        (place.reshape(1, 1), *parts),
        flops=32 * slots * slots,
    )
    table_grad = pl.pallas_call(
        functools.partial(table_kernel, group, per_copy),
        out_shape=b16((ROWS_DEV, width)),
        in_specs=[pl.BlockSpec(memory_space=pltpu.SMEM), vmem(), vmem(), vmem()],
        out_specs=pl.BlockSpec(memory_space=pltpu.HBM),
        scratch_shapes=[
            pltpu.VMEM((slots, slots), jnp.bfloat16),
            pltpu.VMEM((slots, width), jnp.bfloat16),
            pltpu.VMEM((ROWS_DEV, width), jnp.bfloat16),
            pltpu.VMEM((group, width), jnp.float32),
            pltpu.SemaphoreType.DMA((ROWS_DEV // (group * per_copy),)),
        ],
        compiler_params=params(32),
        cost_estimate=pl.CostEstimate(
            flops=2 * slots * slots * width, bytes_accessed=2 * ROWS_DEV * width, transcendentals=0
        ),
    )(got_count.reshape(LANES), got_rows, got_rank, got_sorted)
    return (query_grad, item_grad, table_grad)


def solution(mesh):
    both = P(("blk", "table"), None)
    flat = P(("blk", "table"))
    return jax.shard_map(
        local, mesh=mesh, in_specs=(both, both, flat, both, flat), out_specs=(both, both, both), check_vma=False
    )
```

```python
import functools
import math

import jax
import jax.numpy as jnp
from jax import lax
from jax.experimental import pallas as pl
from jax.experimental.pallas import tpu as pltpu
from jax.sharding import PartitionSpec as P


ROWS_DEV = 16384
LANES = 128
SUB = 256
PACK = 16
RUN = 512
VIEW = 64
LOG2E = math.log2(math.e)
NT = (((1,), (1,)), ((), ()))
TN = (((0,), (0,)), ((), ()))


def moved(block, axis, target_of):
    count = lax.axis_size(axis)
    return lax.ppermute(block, axis, [(i, target_of(i) % count) for i in range(count)])


def vmem():
    return pl.BlockSpec(memory_space=pltpu.VMEM)


def params(mib):
    return pltpu.CompilerParams(vmem_limit_bytes=mib * 2**20)


def call(body, out_shape, args, flops=0, trans=0, mib=12, scratch=()):
    moved_bytes = sum(a.size * a.dtype.itemsize for a in args)
    outs = out_shape if isinstance(out_shape, (tuple, list)) else (out_shape,)
    moved_bytes += sum(math.prod(o.shape) * o.dtype.itemsize for o in outs)
    specs = [pl.BlockSpec(memory_space=pltpu.HBM) if scratch else vmem() for _ in outs]
    return pl.pallas_call(
        body,
        out_shape=out_shape,
        in_specs=[vmem() for _ in args],
        out_specs=specs if isinstance(out_shape, (tuple, list)) else specs[0],
        cost_estimate=pl.CostEstimate(flops=flops, bytes_accessed=moved_bytes, transcendentals=trans),
        compiler_params=params(mib),
        scratch_shapes=scratch,
    )(*args)


def iota(shape, dim, dtype=jnp.int32):
    value = lax.broadcasted_iota(jnp.int32, shape, dim)
    return value if dtype == jnp.int32 else value.astype(dtype)


def column(row):
    wide = jnp.broadcast_to(row, (LANES, LANES))
    return jnp.transpose(wide)


def one_hot(shape, row, base):
    there = (iota(shape, 0) + base).astype(jnp.int16)
    return jnp.where(there == row.astype(jnp.int16), jnp.bfloat16(1), jnp.bfloat16(0))


def first_kernel(devices, capacity, *refs):
    sources, results, (owner_ref, row_ref, done) = refs[:5], refs[5:10], refs[10:]
    slot_ref, ids_ref, pos_ref, q_ref, k_ref = results
    targets = (owner_ref, row_ref, k_ref, q_ref, pos_ref)
    copies = [pltpu.make_async_copy(a, b, done.at[i]) for i, (a, b) in enumerate(zip(sources, targets))]
    for copy in copies:
        copy.start()
    copies[0].wait()
    copies[1].wait()
    route(devices, capacity, owner_ref, row_ref, slot_ref, ids_ref)
    for copy in copies[2:]:
        copy.wait()


def route(devices, capacity, owner_ref, row_ref, slot_ref, ids_ref):
    size = owner_ref.shape[1]
    owner = owner_ref[...]
    rank = jnp.zeros((1, size), jnp.float32)
    for base in range(0, size, LANES):
        col = column(owner[:, base : base + LANES])
        col = jnp.concatenate([col] * (size // LANES), axis=1)
        here = iota((LANES, size), 0) + base
        hit = (col == owner) & (here < iota((LANES, size), 1))
        rank = rank + jnp.sum(jnp.where(hit, 1.0, 0.0), axis=0, keepdims=True)
    rank = rank.astype(jnp.int32)
    slot_ref[...] = owner * capacity + rank
    row = row_ref[...]
    high = (lax.shift_right_logical(row, 7) + 1).astype(jnp.float32)
    low = (row & 127).astype(jnp.float32)
    mine = iota((devices, size), 0) == owner
    place = one_hot((LANES, size), rank, 0)
    high = jnp.where(mine, high, 0.0).astype(jnp.bfloat16)
    low = jnp.where(mine, low, 0.0).astype(jnp.bfloat16)
    high = lax.dot_general(high, place, NT, preferred_element_type=jnp.float32)
    low = lax.dot_general(low, place, NT, preferred_element_type=jnp.float32)
    value = jnp.where(high > 0.5, (high - 1.0) * 128.0 + low, float(ROWS_DEV))
    ids_ref[...] = value.astype(jnp.int32)


def order_kernel(capacity, group, groups, ids_ref, rank_ref, sorted_ref, count_ref):
    devices = ids_ref.shape[0]
    slots = devices * capacity
    chunks = RUN // LANES
    ids = ids_ref[...]
    lane = iota((1, LANES), 1)
    rolled = {}
    rows = [jnp.zeros((1, LANES), jnp.int32) for _ in range(slots // LANES)]
    for s in range(devices):
        at, off = divmod(s * capacity, LANES)
        if off not in rolled:
            rolled[off] = pltpu.roll(ids, off, 1) if off else ids
        piece = rolled[off][s : s + 1, :]
        rows[at] = jnp.where((lane >= off) & (lane < off + capacity), piece, rows[at])
        if off + capacity > LANES:
            rows[at + 1] = jnp.where(lane < off + capacity - LANES, piece, rows[at + 1])
    edges = lane * group
    earlier = iota((LANES, LANES), 0) < iota((LANES, LANES), 1)
    over = jnp.zeros((1, LANES), jnp.float32)
    count_ref[...] = jnp.zeros_like(count_ref)
    for run in range(slots // RUN):
        mine = rows[run * chunks : (run + 1) * chunks]
        count = jnp.zeros((1, LANES), jnp.float32)
        ranks = [jnp.zeros((1, LANES), jnp.float32) for _ in range(chunks)]
        for j in range(chunks):
            col = column(mine[j])
            count = count + jnp.sum(jnp.where(col < edges, 1.0, 0.0), axis=0, keepdims=True)
            for i in range(chunks):
                if j < i:
                    hit = col <= mine[i]
                elif j > i:
                    hit = col < mine[i]
                else:
                    hit = (col < mine[i]) | ((col == mine[i]) & earlier)
                ranks[i] = ranks[i] + jnp.sum(jnp.where(hit, 1.0, 0.0), axis=0, keepdims=True)
        count = count.astype(jnp.int32)
        past = (pltpu.roll(count, LANES - 1, 1) > start_of(count) + VIEW) & (lane < groups)
        over = jnp.maximum(over, jnp.where(past, 1.0, 0.0))
        count_ref[run : run + 1, :] = count
        rank = jnp.concatenate(ranks, axis=1).astype(jnp.int32)
        rank_ref[:, run * RUN : (run + 1) * RUN] = rank
        row = jnp.concatenate(mine, axis=1)
        high = jnp.broadcast_to(lax.shift_right_logical(row, 7).astype(jnp.float32), (8, RUN)).astype(jnp.bfloat16)
        low = jnp.broadcast_to((row & 127).astype(jnp.float32), (8, RUN)).astype(jnp.bfloat16)
        lines = []
        for c in range(chunks):
            pick = one_hot((LANES, RUN), rank, c * LANES)
            up = lax.dot_general(high, pick, NT, preferred_element_type=jnp.float32)
            down = lax.dot_general(low, pick, NT, preferred_element_type=jnp.float32)
            lines.append((up * 128.0 + down)[0:1, :].astype(jnp.int32))
        for o in range(LANES // PACK):
            turned = [pltpu.roll(line, LANES - o * PACK, 1) if o else line for line in lines]
            for c in range(chunks):
                view = jnp.where(lane < LANES - o * PACK, turned[c], turned[min(c + 1, chunks - 1)])
                if run % 2:
                    view = pltpu.roll(view, VIEW, 1)
                sorted_ref[run, o, c : c + 1, :] = view
    over = jnp.max(over, axis=1, keepdims=True).astype(jnp.int32)
    count_ref[0:1, :] = jnp.where(lane == LANES - 1, over, count_ref[0:1, :])


def start_of(count):
    packs = lax.shift_right_logical(count, PACK.bit_length() - 1)
    return jnp.minimum(packs * PACK, RUN - VIEW)


def stats_kernel(scale, blocks, olds, final, *refs):
    q_ref = refs[0]
    k_refs = refs[1 : 1 + blocks]
    old = refs[1 + blocks : 1 + blocks + olds]
    outs = refs[1 + blocks + olds :]
    size = q_ref.shape[0]
    for base in range(0, size, SUB):
        at = slice(base, base + SUB)
        q = q_ref[at, :]
        top = old[0][:, at] if old else None
        total = old[1][:, at] if old else None
        for k in k_refs:
            scores = scale * lax.dot_general(k[...], q, NT, preferred_element_type=jnp.float32)
            high = jnp.max(scores, axis=0, keepdims=True)
            high = high if top is None else jnp.maximum(top, high)
            part = jnp.sum(jnp.exp2(scores - high), axis=0, keepdims=True)
            total = part if top is None else total * jnp.exp2(top - high) + part
            top = high
        if final:
            outs[0][:, at] = top + jnp.log2(total)
        else:
            outs[0][:, at] = top
            outs[1][:, at] = total


def query_kernel(scale, blocks, q_ref, lse_ref, pos_ref, *refs):
    k_refs, out_ref = refs[:blocks], refs[-1]
    size = q_ref.shape[0]
    for base in range(0, size, SUB):
        at = slice(base, base + SUB)
        q = q_ref[at, :]
        total = None
        for m, k in enumerate(k_refs):
            scores = (scale * LOG2E) * lax.dot_general(k[...], q, NT, preferred_element_type=jnp.float32)
            weights = jnp.exp2(scores - lse_ref[:, at])
            if m == 0:
                weights = weights - jnp.where(iota((size, SUB), 0) == pos_ref[:, at], 1.0, 0.0)
            part = lax.dot_general(weights.astype(jnp.bfloat16), k[...], TN, preferred_element_type=jnp.float32)
            total = part if total is None else total + part
        out_ref[at, :] = (scale * total).astype(jnp.bfloat16)


def item_kernel(scale, own, last, k_ref, q_ref, lse_ref, *refs):
    refs = list(refs)
    size = k_ref.shape[0]
    keys = k_ref[...]
    pos = refs.pop(0)[...] if own else None
    total = None if own else refs.pop(0)[...]
    for base in range(0, size, SUB):
        at = slice(base, base + SUB)
        q = q_ref[at, :]
        scores = (scale * LOG2E) * lax.dot_general(keys, q, NT, preferred_element_type=jnp.float32)
        weights = jnp.exp2(scores - lse_ref[:, at])
        if own:
            weights = weights - jnp.where(iota((size, SUB), 0) == pos[:, at], 1.0, 0.0)
        part = jnp.dot(weights.astype(jnp.bfloat16), q, preferred_element_type=jnp.float32)
        total = part if total is None else total + part
    if not last:
        refs[0][...] = total
        return
    slot_ref, out_ref, send_ref, grad_ref, stage_ref, done = refs
    grad = (scale * total).astype(jnp.bfloat16)
    grad_ref[...] = grad
    copies = [pltpu.make_async_copy(grad_ref, out_ref, done.at[0])]
    copies[0].start()
    slots = send_ref.shape[0]
    part = slots // 3 if slots % (3 * SUB) == 0 else slots // 2
    for i, base in enumerate(range(0, slots, part)):
        at = pl.ds(base, part)
        pick = one_hot((part, size), slot_ref[...], base)
        stage_ref[at, :] = jnp.dot(pick, grad, preferred_element_type=jnp.float32).astype(jnp.bfloat16)
        copies.append(pltpu.make_async_copy(stage_ref.at[at, :], send_ref.at[at, :], done.at[1 + i]))
        copies[-1].start()
    for copy in copies:
        copy.wait()


def table_kernel(group, per_copy, count_ref, rows_ref, rank_ref, sorted_ref, out_ref, arranged, table, total, done):
    slots, width = arranged.shape
    groups = table.shape[0] // group
    copies = groups // per_copy
    runs = slots // RUN
    for run in range(runs):
        at = slice(run * RUN, (run + 1) * RUN)
        pick = one_hot((RUN, RUN), rank_ref[:, at], 0)
        arranged[at, :] = jnp.dot(pick, rows_ref[at, :], preferred_element_type=jnp.float32).astype(jnp.bfloat16)

    lane = iota((1, LANES), 1)

    def spread(starts, base):
        views, blocks = [], []
        for run in range(runs):
            start = starts[run]
            turn = lax.shift_right_logical(start, PACK.bit_length() - 1) & (LANES // PACK - 1)
            views.append(sorted_ref[run, turn, pl.ds(lax.shift_right_logical(start, 7), 1), :])
            blocks.append(arranged[pl.ds(pl.multiple_of(run * RUN + start, PACK), VIEW), :])
        if runs % 2:
            views.append(jnp.full((1, LANES), -1, jnp.int32))
            blocks.append(blocks[-1])
        ids = [jnp.where(lane < VIEW, a, b) for a, b in zip(views[::2], views[1::2])]
        ids = jnp.concatenate(ids, axis=1)
        hot = one_hot((group, ids.shape[1]), ids - base, 0)
        return jnp.dot(hot, jnp.concatenate(blocks, axis=0), preferred_element_type=jnp.float32)

    def copy_out(c):
        size = per_copy * group
        at = pl.ds(c * size if isinstance(c, int) else pl.multiple_of(c * size, size), size)
        return pltpu.make_async_copy(table.at[at, :], out_ref.at[at, :], done.at[c])

    over = count_ref[0, LANES - 1] > 0

    @pl.when(jnp.logical_not(over))
    def _():
        for c in range(copies):
            for number in range(c * per_copy, (c + 1) * per_copy):
                starts = [start_of(count_ref[run, number]) for run in range(runs)]
                table[number * group : (number + 1) * group, :] = spread(starts, number * group).astype(jnp.bfloat16)
            copy_out(c).start()

    @pl.when(over)
    def _():
        def one(c, carry):
            def each(g, inner):
                number = c * per_copy + g
                total[...] = jnp.zeros((group, width), jnp.float32)

                def more(part, deeper):
                    total[...] += spread([part * VIEW] * runs, number * group)
                    return deeper

                lax.fori_loop(0, RUN // VIEW, more, 0)
                table[pl.ds(pl.multiple_of(number * group, group), group), :] = total[...].astype(jnp.bfloat16)
                return inner

            lax.fori_loop(0, per_copy, each, 0)
            copy_out(c).start()
            return carry

        lax.fori_loop(0, copies, one, 0)

    for c in range(copies):
        copy_out(c).wait()


def local(queries, items, positives, item_owner, item_row):
    size, width = queries.shape
    scale = 3.0 / math.sqrt(width)
    blk_count = lax.axis_size("blk")
    window = blk_count // 2
    devices = blk_count * lax.axis_size("table")
    capacity = -(-(3 * size // devices) // 8) * 8
    slots = devices * capacity
    f32 = functools.partial(jax.ShapeDtypeStruct, dtype=jnp.float32)
    b16 = functools.partial(jax.ShapeDtypeStruct, dtype=jnp.bfloat16)
    i32 = functools.partial(jax.ShapeDtypeStruct, dtype=jnp.int32)

    owner_row = item_owner.reshape(1, size)
    row_row = item_row.reshape(1, size)
    pos_row = positives.reshape(1, size)

    pair = 2 * size * size * width
    twos = range(1, window // 2)
    k_two = [moved(items, "blk", lambda i, j=j: i + 2 * j) for j in twos]
    k_odd = moved(items, "blk", lambda i: i + window - 1 if i % 2 else i + 1)
    q_two = [moved(queries, "blk", lambda i, j=j: i - 2 * j) for j in twos]
    q_odd = moved(queries, "blk", lambda i: i - 1 if i % 2 else i - (window - 1))
    slot, ids, pos_row, queries, items = pl.pallas_call(
        functools.partial(first_kernel, devices, capacity),
        out_shape=(
            i32((1, size)),
            i32((devices, LANES)),
            i32((1, size)),
            b16((size, width)),
            b16((size, width)),
        ),
        in_specs=[pl.BlockSpec(memory_space=pltpu.HBM) for _ in range(5)],
        out_specs=tuple(vmem() for _ in range(5)),
        scratch_shapes=[
            pltpu.VMEM((1, size), jnp.int32),
            pltpu.VMEM((1, size), jnp.int32),
            pltpu.SemaphoreType.DMA((5,)),
        ],
        compiler_params=params(12),
        cost_estimate=pl.CostEstimate(flops=pair, bytes_accessed=4 * size * width, transcendentals=size * size),
    )(*[pltpu.with_memory_space_constraint(x, pltpu.HBM) for x in (owner_row, row_row, items, queries, pos_row)])
    got_ids = lax.all_to_all(
        ids.reshape(devices, 1, LANES), ("blk", "table"), split_axis=0, concat_axis=0, tiled=True
    ).reshape(devices, LANES)
    k_swap = [moved(k, "blk", lambda i: i ^ 1) for k in k_two]
    q_swap = [moved(q, "blk", lambda i: i ^ 1) for q in q_two]
    k_all = [k_odd, *k_two, *k_swap]
    q_all = [*q_two, q_odd, *q_swap]
    early = [items, k_odd, *k_two]
    top, total = call(
        functools.partial(stats_kernel, scale * LOG2E, len(early), 0, False),
        (f32((1, size)), f32((1, size))),
        (queries, *early),
        flops=pair * len(early),
        trans=size * size * len(early),
    )
    lse = call(
        functools.partial(stats_kernel, scale * LOG2E, len(k_swap), 2, True),
        f32((1, size)),
        (queries, *k_swap, top, total),
        flops=pair * len(k_swap),
        trans=size * size * len(k_swap),
    )
    group, per_copy = 512, 4
    got_rank, got_sorted, got_count = call(
        functools.partial(order_kernel, capacity, group, ROWS_DEV // group),
        (i32((1, slots)), i32((slots // RUN, LANES // PACK, RUN // LANES, LANES)), i32((8, LANES))),
        (got_ids,),
        flops=32 * slots * slots,
    )
    lse_odd = moved(lse, "blk", lambda i: i - 1 if i % 2 else i - (window - 1))
    lse_two = [moved(lse, "blk", lambda i, j=j: i - 2 * j) for j in twos]
    lse_swap = [moved(lse, "blk", lambda i, j=j: (i ^ 1) - 2 * j) for j in twos]
    lse_all = [*lse_two, lse_odd, *lse_swap]

    query_grad = call(
        functools.partial(query_kernel, scale, window),
        b16((size, width)),
        (queries, lse, pos_row, items, *k_all),
        flops=2 * pair * window,
        trans=size * size * window,
    )
    item_sum = call(
        functools.partial(item_kernel, scale, True, False),
        f32((size, width)),
        (items, queries, lse, pos_row),
        flops=2 * pair,
        trans=size * size,
    )
    for q, one in zip(q_all[:-1], lse_all[:-1]):
        item_sum = call(
            functools.partial(item_kernel, scale, False, False),
            f32((size, width)),
            (items, q, one, item_sum),
            flops=2 * pair,
            trans=size * size,
        )
    item_grad, send_rows = call(
        functools.partial(item_kernel, scale, False, True),
        (b16((size, width)), b16((slots, width))),
        (items, q_all[-1], lse_all[-1], item_sum, slot),
        flops=2 * pair + 2 * slots * size * width,
        trans=size * size,
        scratch=[
            pltpu.VMEM((size, width), jnp.bfloat16),
            pltpu.VMEM((slots, width), jnp.bfloat16),
            pltpu.SemaphoreType.DMA((4,)),
        ],
    )
    got_rows = lax.all_to_all(
        send_rows.reshape(devices, capacity, width), ("blk", "table"), split_axis=0, concat_axis=0, tiled=True
    ).reshape(slots, width)
    table_grad = pl.pallas_call(
        functools.partial(table_kernel, group, per_copy),
        out_shape=b16((ROWS_DEV, width)),
        in_specs=[pl.BlockSpec(memory_space=pltpu.SMEM), vmem(), vmem(), vmem()],
        out_specs=pl.BlockSpec(memory_space=pltpu.HBM),
        scratch_shapes=[
            pltpu.VMEM((slots, width), jnp.bfloat16),
            pltpu.VMEM((ROWS_DEV, width), jnp.bfloat16),
            pltpu.VMEM((group, width), jnp.float32),
            pltpu.SemaphoreType.DMA((ROWS_DEV // (group * per_copy),)),
        ],
        compiler_params=params(32),
        cost_estimate=pl.CostEstimate(
            flops=2 * slots * slots * width, bytes_accessed=2 * ROWS_DEV * width, transcendentals=0
        ),
    )(got_count, got_rows, got_rank, got_sorted)
    return (query_grad, item_grad, table_grad)


def solution(mesh):
    both = P(("blk", "table"), None)
    flat = P(("blk", "table"))
    return jax.shard_map(
        local, mesh=mesh, in_specs=(both, both, flat, both, flat), out_specs=(both, both, both), check_vma=False
    )
```

```python
import functools
import math

import jax
import jax.numpy as jnp
from jax import lax
from jax.experimental import pallas as pl
from jax.experimental.pallas import tpu as pltpu
from jax.sharding import PartitionSpec as P


ROWS_DEV = 16384
LANES = 128
SUB = 256
PACK = 16
RUN = 512
VIEW = 64
LOG2E = math.log2(math.e)
NT = (((1,), (1,)), ((), ()))
TN = (((0,), (0,)), ((), ()))


def moved(block, axis, target_of):
    count = lax.axis_size(axis)
    return lax.ppermute(block, axis, [(i, target_of(i) % count) for i in range(count)])


def vmem():
    return pl.BlockSpec(memory_space=pltpu.VMEM)


def params(mib):
    return pltpu.CompilerParams(vmem_limit_bytes=mib * 2**20)


def call(body, out_shape, args, flops=0, trans=0, mib=12, scratch=()):
    moved_bytes = sum(a.size * a.dtype.itemsize for a in args)
    outs = out_shape if isinstance(out_shape, (tuple, list)) else (out_shape,)
    moved_bytes += sum(math.prod(o.shape) * o.dtype.itemsize for o in outs)
    specs = [pl.BlockSpec(memory_space=pltpu.HBM) if scratch else vmem() for _ in outs]
    return pl.pallas_call(
        body,
        out_shape=out_shape,
        in_specs=[vmem() for _ in args],
        out_specs=specs if isinstance(out_shape, (tuple, list)) else specs[0],
        cost_estimate=pl.CostEstimate(flops=flops, bytes_accessed=moved_bytes, transcendentals=trans),
        compiler_params=params(mib),
        scratch_shapes=scratch,
    )(*args)


def iota(shape, dim, dtype=jnp.int32):
    value = lax.broadcasted_iota(jnp.int32, shape, dim)
    return value if dtype == jnp.int32 else value.astype(dtype)


def column(row):
    wide = jnp.broadcast_to(row, (LANES, LANES))
    return jnp.transpose(wide)


def one_hot(shape, row, base):
    there = (iota(shape, 0) + base).astype(jnp.int16)
    return jnp.where(there == row.astype(jnp.int16), jnp.bfloat16(1), jnp.bfloat16(0))


def first_kernel(devices, capacity, *refs):
    sources, results, (owner_ref, row_ref, done) = refs[:5], refs[5:10], refs[10:]
    slot_ref, ids_ref, pos_ref, q_ref, k_ref = results
    targets = (owner_ref, row_ref, k_ref, q_ref, pos_ref)
    copies = [pltpu.make_async_copy(a, b, done.at[i]) for i, (a, b) in enumerate(zip(sources, targets))]
    for copy in copies:
        copy.start()
    copies[0].wait()
    copies[1].wait()
    route(devices, capacity, owner_ref, row_ref, slot_ref, ids_ref)
    for copy in copies[2:]:
        copy.wait()


def route(devices, capacity, owner_ref, row_ref, slot_ref, ids_ref):
    size = owner_ref.shape[1]
    owner = owner_ref[...]
    rank = jnp.zeros((1, size), jnp.float32)
    for base in range(0, size, LANES):
        col = column(owner[:, base : base + LANES])
        col = jnp.concatenate([col] * (size // LANES), axis=1)
        here = iota((LANES, size), 0) + base
        hit = (col == owner) & (here < iota((LANES, size), 1))
        rank = rank + jnp.sum(jnp.where(hit, 1.0, 0.0), axis=0, keepdims=True)
    rank = rank.astype(jnp.int32)
    slot_ref[...] = owner * capacity + rank
    row = row_ref[...]
    high = (lax.shift_right_logical(row, 7) + 1).astype(jnp.float32)
    low = (row & 127).astype(jnp.float32)
    mine = iota((devices, size), 0) == owner
    place = one_hot((LANES, size), rank, 0)
    high = jnp.where(mine, high, 0.0).astype(jnp.bfloat16)
    low = jnp.where(mine, low, 0.0).astype(jnp.bfloat16)
    high = lax.dot_general(high, place, NT, preferred_element_type=jnp.float32)
    low = lax.dot_general(low, place, NT, preferred_element_type=jnp.float32)
    value = jnp.where(high > 0.5, (high - 1.0) * 128.0 + low, float(ROWS_DEV))
    ids_ref[...] = value.astype(jnp.int32)


def order_kernel(capacity, group, groups, ids_ref, rank_ref, sorted_ref, count_ref):
    devices = ids_ref.shape[0]
    slots = devices * capacity
    chunks = RUN // LANES
    ids = ids_ref[...]
    lane = iota((1, LANES), 1)
    rolled = {}
    rows = [jnp.zeros((1, LANES), jnp.int32) for _ in range(slots // LANES)]
    for s in range(devices):
        at, off = divmod(s * capacity, LANES)
        if off not in rolled:
            rolled[off] = pltpu.roll(ids, off, 1) if off else ids
        piece = rolled[off][s : s + 1, :]
        rows[at] = jnp.where((lane >= off) & (lane < off + capacity), piece, rows[at])
        if off + capacity > LANES:
            rows[at + 1] = jnp.where(lane < off + capacity - LANES, piece, rows[at + 1])
    edges = lane * group
    earlier = iota((LANES, LANES), 0) < iota((LANES, LANES), 1)
    over = jnp.zeros((1, LANES), jnp.float32)
    count_ref[...] = jnp.zeros_like(count_ref)
    for run in range(slots // RUN):
        mine = rows[run * chunks : (run + 1) * chunks]
        count = jnp.zeros((1, LANES), jnp.float32)
        ranks = [jnp.zeros((1, LANES), jnp.float32) for _ in range(chunks)]
        for j in range(chunks):
            col = column(mine[j])
            count = count + jnp.sum(jnp.where(col < edges, 1.0, 0.0), axis=0, keepdims=True)
            for i in range(chunks):
                if j < i:
                    hit = col <= mine[i]
                elif j > i:
                    hit = col < mine[i]
                else:
                    hit = (col < mine[i]) | ((col == mine[i]) & earlier)
                ranks[i] = ranks[i] + jnp.sum(jnp.where(hit, 1.0, 0.0), axis=0, keepdims=True)
        count = count.astype(jnp.int32)
        past = (pltpu.roll(count, LANES - 1, 1) > start_of(count) + VIEW) & (lane < groups)
        over = jnp.maximum(over, jnp.where(past, 1.0, 0.0))
        count_ref[run : run + 1, :] = count
        rank = jnp.concatenate(ranks, axis=1).astype(jnp.int32)
        rank_ref[:, run * RUN : (run + 1) * RUN] = rank
        row = jnp.concatenate(mine, axis=1)
        high = jnp.broadcast_to(lax.shift_right_logical(row, 7).astype(jnp.float32), (8, RUN)).astype(jnp.bfloat16)
        low = jnp.broadcast_to((row & 127).astype(jnp.float32), (8, RUN)).astype(jnp.bfloat16)
        lines = []
        for c in range(chunks):
            pick = one_hot((LANES, RUN), rank, c * LANES)
            up = lax.dot_general(high, pick, NT, preferred_element_type=jnp.float32)
            down = lax.dot_general(low, pick, NT, preferred_element_type=jnp.float32)
            lines.append((up * 128.0 + down)[0:1, :].astype(jnp.int32))
        for o in range(LANES // PACK):
            turned = [pltpu.roll(line, LANES - o * PACK, 1) if o else line for line in lines]
            for c in range(chunks):
                view = jnp.where(lane < LANES - o * PACK, turned[c], turned[min(c + 1, chunks - 1)])
                if run % 2:
                    view = pltpu.roll(view, VIEW, 1)
                sorted_ref[run, o, c : c + 1, :] = view
    over = jnp.max(over, axis=1, keepdims=True).astype(jnp.int32)
    count_ref[0:1, :] = jnp.where(lane == LANES - 1, over, count_ref[0:1, :])


def start_of(count):
    packs = lax.shift_right_logical(count, PACK.bit_length() - 1)
    return jnp.minimum(packs * PACK, RUN - VIEW)


def stats_kernel(scale, blocks, olds, final, *refs):
    q_ref = refs[0]
    k_refs = refs[1 : 1 + blocks]
    old = refs[1 + blocks : 1 + blocks + olds]
    outs = refs[1 + blocks + olds :]
    size = q_ref.shape[0]
    for base in range(0, size, SUB):
        at = slice(base, base + SUB)
        q = q_ref[at, :]
        top = old[0][:, at] if old else None
        total = old[1][:, at] if old else None
        for k in k_refs:
            scores = scale * lax.dot_general(k[...], q, NT, preferred_element_type=jnp.float32)
            high = jnp.max(scores, axis=0, keepdims=True)
            high = high if top is None else jnp.maximum(top, high)
            part = jnp.sum(jnp.exp2(scores - high), axis=0, keepdims=True)
            total = part if top is None else total * jnp.exp2(top - high) + part
            top = high
        if final:
            outs[0][:, at] = top + jnp.log2(total)
        else:
            outs[0][:, at] = top
            outs[1][:, at] = total


def query_kernel(scale, blocks, q_ref, lse_ref, pos_ref, *refs):
    k_refs, out_ref = refs[:blocks], refs[-1]
    size = q_ref.shape[0]
    for base in range(0, size, SUB):
        at = slice(base, base + SUB)
        q = q_ref[at, :]
        total = None
        for m, k in enumerate(k_refs):
            scores = (scale * LOG2E) * lax.dot_general(k[...], q, NT, preferred_element_type=jnp.float32)
            weights = jnp.exp2(scores - lse_ref[:, at])
            if m == 0:
                weights = weights - jnp.where(iota((size, SUB), 0) == pos_ref[:, at], 1.0, 0.0)
            part = lax.dot_general(weights.astype(jnp.bfloat16), k[...], TN, preferred_element_type=jnp.float32)
            total = part if total is None else total + part
        out_ref[at, :] = (scale * total).astype(jnp.bfloat16)


def item_terms(scale, keys, q_refs, lse_refs, total, pos=None):
    size = keys.shape[0]
    for q_ref, lse_ref in zip(q_refs, lse_refs):
        for base in range(0, size, SUB):
            at = slice(base, base + SUB)
            q = q_ref[at, :]
            scores = (scale * LOG2E) * lax.dot_general(keys, q, NT, preferred_element_type=jnp.float32)
            weights = jnp.exp2(scores - lse_ref[:, at])
            if pos is not None:
                weights = weights - jnp.where(iota((size, SUB), 0) == pos[:, at], 1.0, 0.0)
            part = jnp.dot(weights.astype(jnp.bfloat16), q, preferred_element_type=jnp.float32)
            total = part if total is None else total + part
    return total


def own_kernel(scale, k_ref, q_ref, lse_ref, pos_ref, out_ref):
    out_ref[...] = item_terms(scale, k_ref[...], [q_ref], [lse_ref], None, pos_ref[...])


def more_kernel(scale, blocks, k_ref, sum_ref, *refs):
    refs[-1][...] = item_terms(scale, k_ref[...], refs[:blocks], refs[blocks : 2 * blocks], sum_ref[...])


def item_kernel(scale, blocks, k_ref, slot_ref, sum_ref, *refs):
    q_refs, lse_refs = refs[:blocks], refs[blocks : 2 * blocks]
    out_ref, send_ref, grad_ref, stage_ref, done = refs[2 * blocks :]
    size = k_ref.shape[0]
    total = item_terms(scale, k_ref[...], q_refs, lse_refs, sum_ref[...])
    grad = (scale * total).astype(jnp.bfloat16)
    grad_ref[...] = grad
    copies = [pltpu.make_async_copy(grad_ref, out_ref, done.at[0])]
    copies[0].start()
    slots = send_ref.shape[0]
    part = slots // 3 if slots % (3 * SUB) == 0 else slots // 2
    for i, base in enumerate(range(0, slots, part)):
        at = pl.ds(base, part)
        pick = one_hot((part, size), slot_ref[...], base)
        stage_ref[at, :] = jnp.dot(pick, grad, preferred_element_type=jnp.float32).astype(jnp.bfloat16)
        copies.append(pltpu.make_async_copy(stage_ref.at[at, :], send_ref.at[at, :], done.at[1 + i]))
        copies[-1].start()
    for copy in copies:
        copy.wait()


def table_kernel(group, per_copy, count_ref, rows_ref, rank_ref, sorted_ref, out_ref, arranged, table, total, done):
    slots, width = arranged.shape
    groups = table.shape[0] // group
    copies = groups // per_copy
    runs = slots // RUN
    for run in range(runs):
        at = slice(run * RUN, (run + 1) * RUN)
        pick = one_hot((RUN, RUN), rank_ref[:, at], 0)
        arranged[at, :] = jnp.dot(pick, rows_ref[at, :], preferred_element_type=jnp.float32).astype(jnp.bfloat16)

    lane = iota((1, LANES), 1)

    def spread(starts, base):
        views, blocks = [], []
        for run in range(runs):
            start = starts[run]
            turn = lax.shift_right_logical(start, PACK.bit_length() - 1) & (LANES // PACK - 1)
            views.append(sorted_ref[run, turn, pl.ds(lax.shift_right_logical(start, 7), 1), :])
            blocks.append(arranged[pl.ds(pl.multiple_of(run * RUN + start, PACK), VIEW), :])
        if runs % 2:
            views.append(jnp.full((1, LANES), -1, jnp.int32))
            blocks.append(blocks[-1])
        ids = [jnp.where(lane < VIEW, a, b) for a, b in zip(views[::2], views[1::2])]
        ids = jnp.concatenate(ids, axis=1)
        hot = one_hot((group, ids.shape[1]), ids - base, 0)
        return jnp.dot(hot, jnp.concatenate(blocks, axis=0), preferred_element_type=jnp.float32)

    def copy_out(c):
        size = per_copy * group
        at = pl.ds(c * size if isinstance(c, int) else pl.multiple_of(c * size, size), size)
        return pltpu.make_async_copy(table.at[at, :], out_ref.at[at, :], done.at[c])

    over = count_ref[0, LANES - 1] > 0

    @pl.when(jnp.logical_not(over))
    def _():
        for c in range(copies):
            for number in range(c * per_copy, (c + 1) * per_copy):
                starts = [start_of(count_ref[run, number]) for run in range(runs)]
                table[number * group : (number + 1) * group, :] = spread(starts, number * group).astype(jnp.bfloat16)
            copy_out(c).start()

    @pl.when(over)
    def _():
        def one(c, carry):
            def each(g, inner):
                number = c * per_copy + g
                total[...] = jnp.zeros((group, width), jnp.float32)

                def more(part, deeper):
                    total[...] += spread([part * VIEW] * runs, number * group)
                    return deeper

                lax.fori_loop(0, RUN // VIEW, more, 0)
                table[pl.ds(pl.multiple_of(number * group, group), group), :] = total[...].astype(jnp.bfloat16)
                return inner

            lax.fori_loop(0, per_copy, each, 0)
            copy_out(c).start()
            return carry

        lax.fori_loop(0, copies, one, 0)

    for c in range(copies):
        copy_out(c).wait()


def local(queries, items, positives, item_owner, item_row):
    size, width = queries.shape
    scale = 3.0 / math.sqrt(width)
    blk_count = lax.axis_size("blk")
    window = blk_count // 2
    devices = blk_count * lax.axis_size("table")
    capacity = -(-(3 * size // devices) // 8) * 8
    slots = devices * capacity
    f32 = functools.partial(jax.ShapeDtypeStruct, dtype=jnp.float32)
    b16 = functools.partial(jax.ShapeDtypeStruct, dtype=jnp.bfloat16)
    i32 = functools.partial(jax.ShapeDtypeStruct, dtype=jnp.int32)

    owner_row = item_owner.reshape(1, size)
    row_row = item_row.reshape(1, size)
    pos_row = positives.reshape(1, size)

    pair = 2 * size * size * width
    twos = range(1, window // 2)
    k_two = [moved(items, "blk", lambda i, j=j: i + 2 * j) for j in twos]
    k_odd = moved(items, "blk", lambda i: i + window - 1 if i % 2 else i + 1)
    q_two = [moved(queries, "blk", lambda i, j=j: i - 2 * j) for j in twos]
    q_odd = moved(queries, "blk", lambda i: i - 1 if i % 2 else i - (window - 1))
    slot, ids, pos_row, queries, items = pl.pallas_call(
        functools.partial(first_kernel, devices, capacity),
        out_shape=(
            i32((1, size)),
            i32((devices, LANES)),
            i32((1, size)),
            b16((size, width)),
            b16((size, width)),
        ),
        in_specs=[pl.BlockSpec(memory_space=pltpu.HBM) for _ in range(5)],
        out_specs=tuple(vmem() for _ in range(5)),
        scratch_shapes=[
            pltpu.VMEM((1, size), jnp.int32),
            pltpu.VMEM((1, size), jnp.int32),
            pltpu.SemaphoreType.DMA((5,)),
        ],
        compiler_params=params(12),
        cost_estimate=pl.CostEstimate(flops=pair, bytes_accessed=4 * size * width, transcendentals=size * size),
    )(*[pltpu.with_memory_space_constraint(x, pltpu.HBM) for x in (owner_row, row_row, items, queries, pos_row)])
    got_ids = lax.all_to_all(
        ids.reshape(devices, 1, LANES), ("blk", "table"), split_axis=0, concat_axis=0, tiled=True
    ).reshape(devices, LANES)
    k_swap = [moved(k, "blk", lambda i: i ^ 1) for k in k_two]
    q_swap = [moved(q, "blk", lambda i: i ^ 1) for q in q_two]
    k_all = [k_odd, *k_two, *k_swap]
    q_all = [*q_two, q_odd, *q_swap]
    early = [items, k_odd, *k_two]
    top, total = call(
        functools.partial(stats_kernel, scale * LOG2E, len(early), 0, False),
        (f32((1, size)), f32((1, size))),
        (queries, *early),
        flops=pair * len(early),
        trans=size * size * len(early),
    )
    lse = call(
        functools.partial(stats_kernel, scale * LOG2E, len(k_swap), 2, True),
        f32((1, size)),
        (queries, *k_swap, top, total),
        flops=pair * len(k_swap),
        trans=size * size * len(k_swap),
    )
    group, per_copy = 512, 2
    got_rank, got_sorted, got_count = call(
        functools.partial(order_kernel, capacity, group, ROWS_DEV // group),
        (i32((1, slots)), i32((slots // RUN, LANES // PACK, RUN // LANES, LANES)), i32((8, LANES))),
        (got_ids,),
        flops=32 * slots * slots,
    )
    lse_odd = moved(lse, "blk", lambda i: i - 1 if i % 2 else i - (window - 1))
    lse_two = [moved(lse, "blk", lambda i, j=j: i - 2 * j) for j in twos]
    lse_swap = [moved(one, "blk", lambda i: i ^ 1) for one in lse_two]
    lse_all = [*lse_two, lse_odd, *lse_swap]

    query_grad = call(
        functools.partial(query_kernel, scale, window),
        b16((size, width)),
        (queries, lse, pos_row, items, *k_all),
        flops=2 * pair * window,
        trans=size * size * window,
    )
    item_sum = call(
        functools.partial(own_kernel, scale),
        f32((size, width)),
        (items, queries, lse, pos_row),
        flops=2 * pair,
        trans=size * size,
    )
    cut = len(q_all) - len(q_swap)
    item_sum = call(
        functools.partial(more_kernel, scale, cut),
        f32((size, width)),
        (items, item_sum, *q_all[:cut], *lse_all[:cut]),
        flops=2 * pair * cut,
        trans=size * size * cut,
    )
    item_grad, send_rows = call(
        functools.partial(item_kernel, scale, len(q_swap)),
        (b16((size, width)), b16((slots, width))),
        (items, slot, item_sum, *q_all[cut:], *lse_all[cut:]),
        flops=2 * pair * len(q_swap) + 2 * slots * size * width,
        trans=size * size * len(q_swap),
        scratch=[
            pltpu.VMEM((size, width), jnp.bfloat16),
            pltpu.VMEM((slots, width), jnp.bfloat16),
            pltpu.SemaphoreType.DMA((4,)),
        ],
    )
    got_rows = lax.all_to_all(
        send_rows.reshape(devices, capacity, width), ("blk", "table"), split_axis=0, concat_axis=0, tiled=True
    ).reshape(slots, width)
    table_grad = pl.pallas_call(
        functools.partial(table_kernel, group, per_copy),
        out_shape=b16((ROWS_DEV, width)),
        in_specs=[pl.BlockSpec(memory_space=pltpu.SMEM), vmem(), vmem(), vmem()],
        out_specs=pl.BlockSpec(memory_space=pltpu.HBM),
        scratch_shapes=[
            pltpu.VMEM((slots, width), jnp.bfloat16),
            pltpu.VMEM((ROWS_DEV, width), jnp.bfloat16),
            pltpu.VMEM((group, width), jnp.float32),
            pltpu.SemaphoreType.DMA((ROWS_DEV // (group * per_copy),)),
        ],
        compiler_params=params(32),
        cost_estimate=pl.CostEstimate(
            flops=2 * slots * slots * width, bytes_accessed=2 * ROWS_DEV * width, transcendentals=0
        ),
    )(got_count, got_rows, got_rank, got_sorted)
    return (query_grad, item_grad, table_grad)


def solution(mesh):
    both = P(("blk", "table"), None)
    flat = P(("blk", "table"))
    return jax.shard_map(
        local, mesh=mesh, in_specs=(both, both, flat, both, flat), out_specs=(both, both, both), check_vma=False
    )
```

```python
import functools
import math

import jax
import jax.numpy as jnp
from jax import lax
from jax.experimental import pallas as pl
from jax.experimental.pallas import tpu as pltpu
from jax.sharding import PartitionSpec as P


ROWS_DEV = 16384
LANES = 128
SUB = 256
PACK = 16
RUN = 512
VIEW = 64
LOG2E = math.log2(math.e)
NT = (((1,), (1,)), ((), ()))
TN = (((0,), (0,)), ((), ()))


def moved(block, axis, target_of):
    count = lax.axis_size(axis)
    return lax.ppermute(block, axis, [(i, target_of(i) % count) for i in range(count)])


def vmem():
    return pl.BlockSpec(memory_space=pltpu.VMEM)


def params(mib):
    return pltpu.CompilerParams(vmem_limit_bytes=mib * 2**20)


def call(body, out_shape, args, flops=0, trans=0, mib=12, scratch=()):
    moved_bytes = sum(a.size * a.dtype.itemsize for a in args)
    outs = out_shape if isinstance(out_shape, (tuple, list)) else (out_shape,)
    moved_bytes += sum(math.prod(o.shape) * o.dtype.itemsize for o in outs)
    specs = [pl.BlockSpec(memory_space=pltpu.HBM) if scratch else vmem() for _ in outs]
    return pl.pallas_call(
        body,
        out_shape=out_shape,
        in_specs=[vmem() for _ in args],
        out_specs=specs if isinstance(out_shape, (tuple, list)) else specs[0],
        cost_estimate=pl.CostEstimate(flops=flops, bytes_accessed=moved_bytes, transcendentals=trans),
        compiler_params=params(mib),
        scratch_shapes=scratch,
    )(*args)


def iota(shape, dim, dtype=jnp.int32):
    value = lax.broadcasted_iota(jnp.int32, shape, dim)
    return value if dtype == jnp.int32 else value.astype(dtype)


def column(row):
    wide = jnp.broadcast_to(row, (LANES, LANES))
    return jnp.transpose(wide)


def one_hot(shape, row, base):
    there = (iota(shape, 0) + base).astype(jnp.int16)
    return jnp.where(there == row.astype(jnp.int16), jnp.bfloat16(1), jnp.bfloat16(0))


def first_kernel(devices, tables, capacity, *refs):
    sources, results, (owner_ref, row_ref, done) = refs[:5], refs[5:10], refs[10:]
    slot_ref, ids_ref, pos_ref, q_ref, k_ref = results
    targets = (owner_ref, row_ref, k_ref, q_ref, pos_ref)
    copies = [pltpu.make_async_copy(a, b, done.at[i]) for i, (a, b) in enumerate(zip(sources, targets))]
    for copy in copies:
        copy.start()
    copies[0].wait()
    copies[1].wait()
    route(devices, tables, capacity, owner_ref, row_ref, slot_ref, ids_ref)
    for copy in copies[2:]:
        copy.wait()


def route(devices, tables, capacity, owner_ref, row_ref, slot_ref, ids_ref):
    size = owner_ref.shape[1]
    owner = owner_ref[...]
    owner = lax.rem(owner, tables) * (devices // tables) + lax.div(owner, tables)
    rank = jnp.zeros((1, size), jnp.float32)
    for base in range(0, size, LANES):
        col = column(owner[:, base : base + LANES])
        col = jnp.concatenate([col] * (size // LANES), axis=1)
        here = iota((LANES, size), 0) + base
        hit = (col == owner) & (here < iota((LANES, size), 1))
        rank = rank + jnp.sum(jnp.where(hit, 1.0, 0.0), axis=0, keepdims=True)
    rank = rank.astype(jnp.int32)
    slot_ref[...] = owner * capacity + rank
    row = row_ref[...]
    high = (lax.shift_right_logical(row, 7) + 1).astype(jnp.float32)
    low = (row & 127).astype(jnp.float32)
    mine = iota((devices, size), 0) == owner
    place = one_hot((LANES, size), rank, 0)
    high = jnp.where(mine, high, 0.0).astype(jnp.bfloat16)
    low = jnp.where(mine, low, 0.0).astype(jnp.bfloat16)
    high = lax.dot_general(high, place, NT, preferred_element_type=jnp.float32)
    low = lax.dot_general(low, place, NT, preferred_element_type=jnp.float32)
    value = jnp.where(high > 0.5, (high - 1.0) * 128.0 + low, float(ROWS_DEV))
    ids_ref[...] = value.astype(jnp.int32)


def order_kernel(capacity, group, groups, ids_ref, rank_ref, sorted_ref, count_ref):
    devices = ids_ref.shape[0]
    slots = devices * capacity
    chunks = RUN // LANES
    ids = ids_ref[...]
    lane = iota((1, LANES), 1)
    rolled = {}
    rows = [jnp.zeros((1, LANES), jnp.int32) for _ in range(slots // LANES)]
    for s in range(devices):
        at, off = divmod(s * capacity, LANES)
        if off not in rolled:
            rolled[off] = pltpu.roll(ids, off, 1) if off else ids
        piece = rolled[off][s : s + 1, :]
        rows[at] = jnp.where((lane >= off) & (lane < off + capacity), piece, rows[at])
        if off + capacity > LANES:
            rows[at + 1] = jnp.where(lane < off + capacity - LANES, piece, rows[at + 1])
    edges = lane * group
    earlier = iota((LANES, LANES), 0) < iota((LANES, LANES), 1)
    over = jnp.zeros((1, LANES), jnp.float32)
    count_ref[...] = jnp.zeros_like(count_ref)
    for run in range(slots // RUN):
        mine = rows[run * chunks : (run + 1) * chunks]
        count = jnp.zeros((1, LANES), jnp.float32)
        ranks = [jnp.zeros((1, LANES), jnp.float32) for _ in range(chunks)]
        for j in range(chunks):
            col = column(mine[j])
            count = count + jnp.sum(jnp.where(col < edges, 1.0, 0.0), axis=0, keepdims=True)
            for i in range(chunks):
                if j < i:
                    hit = col <= mine[i]
                elif j > i:
                    hit = col < mine[i]
                else:
                    hit = (col < mine[i]) | ((col == mine[i]) & earlier)
                ranks[i] = ranks[i] + jnp.sum(jnp.where(hit, 1.0, 0.0), axis=0, keepdims=True)
        count = count.astype(jnp.int32)
        past = (pltpu.roll(count, LANES - 1, 1) > start_of(count) + VIEW) & (lane < groups)
        over = jnp.maximum(over, jnp.where(past, 1.0, 0.0))
        count_ref[run : run + 1, :] = count
        rank = jnp.concatenate(ranks, axis=1).astype(jnp.int32)
        rank_ref[:, run * RUN : (run + 1) * RUN] = rank
        row = jnp.concatenate(mine, axis=1)
        high = jnp.broadcast_to(lax.shift_right_logical(row, 7).astype(jnp.float32), (8, RUN)).astype(jnp.bfloat16)
        low = jnp.broadcast_to((row & 127).astype(jnp.float32), (8, RUN)).astype(jnp.bfloat16)
        lines = []
        for c in range(chunks):
            pick = one_hot((LANES, RUN), rank, c * LANES)
            up = lax.dot_general(high, pick, NT, preferred_element_type=jnp.float32)
            down = lax.dot_general(low, pick, NT, preferred_element_type=jnp.float32)
            lines.append((up * 128.0 + down)[0:1, :].astype(jnp.int32))
        for o in range(LANES // PACK):
            turned = [pltpu.roll(line, LANES - o * PACK, 1) if o else line for line in lines]
            for c in range(chunks):
                view = jnp.where(lane < LANES - o * PACK, turned[c], turned[min(c + 1, chunks - 1)])
                if run % 2:
                    view = pltpu.roll(view, VIEW, 1)
                sorted_ref[run, o, c : c + 1, :] = view
    over = jnp.max(over, axis=1, keepdims=True).astype(jnp.int32)
    count_ref[0:1, :] = jnp.where(lane == LANES - 1, over, count_ref[0:1, :])


def start_of(count):
    packs = lax.shift_right_logical(count, PACK.bit_length() - 1)
    return jnp.minimum(packs * PACK, RUN - VIEW)


def stats_kernel(scale, blocks, olds, final, *refs):
    q_ref = refs[0]
    k_refs = refs[1 : 1 + blocks]
    old = refs[1 + blocks : 1 + blocks + olds]
    outs = refs[1 + blocks + olds :]
    size = q_ref.shape[0]
    for base in range(0, size, SUB):
        at = slice(base, base + SUB)
        q = q_ref[at, :]
        top = old[0][:, at] if old else None
        total = old[1][:, at] if old else None
        for k in k_refs:
            scores = scale * lax.dot_general(k[...], q, NT, preferred_element_type=jnp.float32)
            high = jnp.max(scores, axis=0, keepdims=True)
            high = high if top is None else jnp.maximum(top, high)
            part = jnp.sum(jnp.exp2(scores - high), axis=0, keepdims=True)
            total = part if top is None else total * jnp.exp2(top - high) + part
            top = high
        if final:
            outs[0][:, at] = top + jnp.log2(total)
        else:
            outs[0][:, at] = top
            outs[1][:, at] = total


def query_kernel(scale, blocks, q_ref, lse_ref, pos_ref, *refs):
    k_refs, out_ref = refs[:blocks], refs[-1]
    size = q_ref.shape[0]
    for base in range(0, size, SUB):
        at = slice(base, base + SUB)
        q = q_ref[at, :]
        total = None
        for m, k in enumerate(k_refs):
            scores = (scale * LOG2E) * lax.dot_general(k[...], q, NT, preferred_element_type=jnp.float32)
            weights = jnp.exp2(scores - lse_ref[:, at])
            if m == 0:
                weights = weights - jnp.where(iota((size, SUB), 0) == pos_ref[:, at], 1.0, 0.0)
            part = lax.dot_general(weights.astype(jnp.bfloat16), k[...], TN, preferred_element_type=jnp.float32)
            total = part if total is None else total + part
        out_ref[at, :] = (scale * total).astype(jnp.bfloat16)


def item_terms(scale, keys, q_refs, lse_refs, total, pos=None):
    size = keys.shape[0]
    for q_ref, lse_ref in zip(q_refs, lse_refs):
        for base in range(0, size, SUB):
            at = slice(base, base + SUB)
            q = q_ref[at, :]
            scores = (scale * LOG2E) * lax.dot_general(keys, q, NT, preferred_element_type=jnp.float32)
            weights = jnp.exp2(scores - lse_ref[:, at])
            if pos is not None:
                weights = weights - jnp.where(iota((size, SUB), 0) == pos[:, at], 1.0, 0.0)
            part = jnp.dot(weights.astype(jnp.bfloat16), q, preferred_element_type=jnp.float32)
            total = part if total is None else total + part
    return total


def own_kernel(scale, k_ref, q_ref, lse_ref, pos_ref, out_ref):
    out_ref[...] = item_terms(scale, k_ref[...], [q_ref], [lse_ref], None, pos_ref[...])


def more_kernel(scale, blocks, k_ref, sum_ref, *refs):
    refs[-1][...] = item_terms(scale, k_ref[...], refs[:blocks], refs[blocks : 2 * blocks], sum_ref[...])


def item_kernel(scale, blocks, k_ref, slot_ref, sum_ref, *refs):
    q_refs, lse_refs = refs[:blocks], refs[blocks : 2 * blocks]
    out_ref, send_ref, grad_ref, stage_ref, done = refs[2 * blocks :]
    size = k_ref.shape[0]
    total = item_terms(scale, k_ref[...], q_refs, lse_refs, sum_ref[...])
    grad = (scale * total).astype(jnp.bfloat16)
    grad_ref[...] = grad
    copies = [pltpu.make_async_copy(grad_ref, out_ref, done.at[0])]
    copies[0].start()
    slots = send_ref.shape[0]
    part = slots // 3 if slots % (3 * SUB) == 0 else slots // 2
    for i, base in enumerate(range(0, slots, part)):
        at = pl.ds(base, part)
        pick = one_hot((part, size), slot_ref[...], base)
        stage_ref[at, :] = jnp.dot(pick, grad, preferred_element_type=jnp.float32).astype(jnp.bfloat16)
        copies.append(pltpu.make_async_copy(stage_ref.at[at, :], send_ref.at[at, :], done.at[1 + i]))
        copies[-1].start()
    for copy in copies:
        copy.wait()


def table_kernel(group, per_copy, count_ref, rows_ref, rank_ref, sorted_ref, out_ref, arranged, table, total, done):
    slots, width = arranged.shape
    groups = table.shape[0] // group
    copies = groups // per_copy
    runs = slots // RUN
    for run in range(runs):
        at = slice(run * RUN, (run + 1) * RUN)
        pick = one_hot((RUN, RUN), rank_ref[:, at], 0)
        arranged[at, :] = jnp.dot(pick, rows_ref[at, :], preferred_element_type=jnp.float32).astype(jnp.bfloat16)

    lane = iota((1, LANES), 1)

    def spread(starts, base):
        views, blocks = [], []
        for run in range(runs):
            start = starts[run]
            turn = lax.shift_right_logical(start, PACK.bit_length() - 1) & (LANES // PACK - 1)
            views.append(sorted_ref[run, turn, pl.ds(lax.shift_right_logical(start, 7), 1), :])
            blocks.append(arranged[pl.ds(pl.multiple_of(run * RUN + start, PACK), VIEW), :])
        if runs % 2:
            views.append(jnp.full((1, LANES), -1, jnp.int32))
            blocks.append(blocks[-1])
        ids = [jnp.where(lane < VIEW, a, b) for a, b in zip(views[::2], views[1::2])]
        ids = jnp.concatenate(ids, axis=1)
        hot = one_hot((group, ids.shape[1]), ids - base, 0)
        return jnp.dot(hot, jnp.concatenate(blocks, axis=0), preferred_element_type=jnp.float32)

    def copy_out(c):
        size = per_copy * group
        at = pl.ds(c * size if isinstance(c, int) else pl.multiple_of(c * size, size), size)
        return pltpu.make_async_copy(table.at[at, :], out_ref.at[at, :], done.at[c])

    over = count_ref[0, LANES - 1] > 0

    @pl.when(jnp.logical_not(over))
    def _():
        for c in range(copies):
            for number in range(c * per_copy, (c + 1) * per_copy):
                starts = [start_of(count_ref[run, number]) for run in range(runs)]
                table[number * group : (number + 1) * group, :] = spread(starts, number * group).astype(jnp.bfloat16)
            copy_out(c).start()

    @pl.when(over)
    def _():
        def one(c, carry):
            def each(g, inner):
                number = c * per_copy + g
                total[...] = jnp.zeros((group, width), jnp.float32)

                def more(part, deeper):
                    total[...] += spread([part * VIEW] * runs, number * group)
                    return deeper

                lax.fori_loop(0, RUN // VIEW, more, 0)
                table[pl.ds(pl.multiple_of(number * group, group), group), :] = total[...].astype(jnp.bfloat16)
                return inner

            lax.fori_loop(0, per_copy, each, 0)
            copy_out(c).start()
            return carry

        lax.fori_loop(0, copies, one, 0)

    for c in range(copies):
        copy_out(c).wait()


def local(queries, items, positives, item_owner, item_row):
    size, width = queries.shape
    scale = 3.0 / math.sqrt(width)
    blk_count = lax.axis_size("blk")
    window = blk_count // 2
    devices = blk_count * lax.axis_size("table")
    capacity = -(-(3 * size // devices) // 8) * 8
    slots = devices * capacity
    f32 = functools.partial(jax.ShapeDtypeStruct, dtype=jnp.float32)
    b16 = functools.partial(jax.ShapeDtypeStruct, dtype=jnp.bfloat16)
    i32 = functools.partial(jax.ShapeDtypeStruct, dtype=jnp.int32)

    owner_row = item_owner.reshape(1, size)
    row_row = item_row.reshape(1, size)
    pos_row = positives.reshape(1, size)

    pair = 2 * size * size * width
    twos = range(1, window // 2)
    k_two = [moved(items, "blk", lambda i, j=j: i + 2 * j) for j in twos]
    k_odd = moved(items, "blk", lambda i: i + window - 1 if i % 2 else i + 1)
    q_two = [moved(queries, "blk", lambda i, j=j: i - 2 * j) for j in twos]
    q_odd = moved(queries, "blk", lambda i: i - 1 if i % 2 else i - (window - 1))
    slot, ids, pos_row, queries, items = pl.pallas_call(
        functools.partial(first_kernel, devices, lax.axis_size("table"), capacity),
        out_shape=(
            i32((1, size)),
            i32((devices, LANES)),
            i32((1, size)),
            b16((size, width)),
            b16((size, width)),
        ),
        in_specs=[pl.BlockSpec(memory_space=pltpu.HBM) for _ in range(5)],
        out_specs=tuple(vmem() for _ in range(5)),
        scratch_shapes=[
            pltpu.VMEM((1, size), jnp.int32),
            pltpu.VMEM((1, size), jnp.int32),
            pltpu.SemaphoreType.DMA((5,)),
        ],
        compiler_params=params(12),
        cost_estimate=pl.CostEstimate(flops=pair, bytes_accessed=4 * size * width, transcendentals=size * size),
    )(*[pltpu.with_memory_space_constraint(x, pltpu.HBM) for x in (owner_row, row_row, items, queries, pos_row)])
    got_ids = lax.all_to_all(
        ids.reshape(devices, 1, LANES), ("table", "blk"), split_axis=0, concat_axis=0, tiled=True
    ).reshape(devices, LANES)
    k_swap = [moved(k, "blk", lambda i: i ^ 1) for k in k_two]
    q_swap = [moved(q, "blk", lambda i: i ^ 1) for q in q_two]
    k_all = [k_odd, *k_two, *k_swap]
    q_all = [*q_two, q_odd, *q_swap]
    early = [items, k_odd, *k_two]
    top, total = call(
        functools.partial(stats_kernel, scale * LOG2E, len(early), 0, False),
        (f32((1, size)), f32((1, size))),
        (queries, *early),
        flops=pair * len(early),
        trans=size * size * len(early),
    )
    lse = call(
        functools.partial(stats_kernel, scale * LOG2E, len(k_swap), 2, True),
        f32((1, size)),
        (queries, *k_swap, top, total),
        flops=pair * len(k_swap),
        trans=size * size * len(k_swap),
    )
    group, per_copy = 512, 2
    got_rank, got_sorted, got_count = call(
        functools.partial(order_kernel, capacity, group, ROWS_DEV // group),
        (i32((1, slots)), i32((slots // RUN, LANES // PACK, RUN // LANES, LANES)), i32((8, LANES))),
        (got_ids,),
        flops=32 * slots * slots,
    )
    lse_odd = moved(lse, "blk", lambda i: i - 1 if i % 2 else i - (window - 1))
    lse_two = [moved(lse, "blk", lambda i, j=j: i - 2 * j) for j in twos]
    lse_swap = [moved(one, "blk", lambda i: i ^ 1) for one in lse_two]
    lse_all = [*lse_two, lse_odd, *lse_swap]

    query_grad = call(
        functools.partial(query_kernel, scale, window),
        b16((size, width)),
        (queries, lse, pos_row, items, *k_all),
        flops=2 * pair * window,
        trans=size * size * window,
    )
    item_sum = call(
        functools.partial(own_kernel, scale),
        f32((size, width)),
        (items, queries, lse, pos_row),
        flops=2 * pair,
        trans=size * size,
    )
    cut = len(q_all) - len(q_swap)
    item_sum = call(
        functools.partial(more_kernel, scale, cut),
        f32((size, width)),
        (items, item_sum, *q_all[:cut], *lse_all[:cut]),
        flops=2 * pair * cut,
        trans=size * size * cut,
    )
    item_grad, send_rows = call(
        functools.partial(item_kernel, scale, len(q_swap)),
        (b16((size, width)), b16((slots, width))),
        (items, slot, item_sum, *q_all[cut:], *lse_all[cut:]),
        flops=2 * pair * len(q_swap) + 2 * slots * size * width,
        trans=size * size * len(q_swap),
        scratch=[
            pltpu.VMEM((size, width), jnp.bfloat16),
            pltpu.VMEM((slots, width), jnp.bfloat16),
            pltpu.SemaphoreType.DMA((4,)),
        ],
    )
    got_rows = lax.all_to_all(
        send_rows.reshape(devices, capacity, width), ("table", "blk"), split_axis=0, concat_axis=0, tiled=True
    ).reshape(slots, width)
    table_grad = pl.pallas_call(
        functools.partial(table_kernel, group, per_copy),
        out_shape=b16((ROWS_DEV, width)),
        in_specs=[pl.BlockSpec(memory_space=pltpu.SMEM), vmem(), vmem(), vmem()],
        out_specs=pl.BlockSpec(memory_space=pltpu.HBM),
        scratch_shapes=[
            pltpu.VMEM((slots, width), jnp.bfloat16),
            pltpu.VMEM((ROWS_DEV, width), jnp.bfloat16),
            pltpu.VMEM((group, width), jnp.float32),
            pltpu.SemaphoreType.DMA((ROWS_DEV // (group * per_copy),)),
        ],
        compiler_params=params(32),
        cost_estimate=pl.CostEstimate(
            flops=2 * slots * slots * width, bytes_accessed=2 * ROWS_DEV * width, transcendentals=0
        ),
    )(got_count, got_rows, got_rank, got_sorted)
    return (query_grad, item_grad, table_grad)


def solution(mesh):
    both = P(("blk", "table"), None)
    flat = P(("blk", "table"))
    return jax.shard_map(
        local, mesh=mesh, in_specs=(both, both, flat, both, flat), out_specs=(both, both, both), check_vma=False
    )
```
